256 devices in a mesh: snap: 8 (over y, core), vtx: 32 (over z, x).
Axes of the slice: x: 4, y: 4, z: 8, core: 2. Of those that a mesh axis runs over, the one named last changes fastest.
Arguments:
- features: bfloat16 [16, 32768, 128], P('snap', 'vtx'), may hold values from -6 to 6
- tile_vals: bfloat16 [16, 256, 16, 128, 128], P('snap', 'vtx'), may hold values from -0.25 to 0.25
- tile_cols: int32 [16, 256, 16], P('snap', 'vtx'), may hold values from 0 to 255, as said below
- tile_count: int32 [16, 256], P('snap', 'vtx'), may hold values from 1 to 16
- gcn_weight: bfloat16 [128, 128], replicated, may hold values from -0.5 to 0.5
- gcn_bias: float32 [128], replicated, may hold values from -3 to 3
- input_weight: bfloat16 [128, 512], replicated, may hold values from -0.5 to 0.5
- recur_weight: bfloat16 [128, 512], replicated, may hold values from -0.5 to 0.5
- lstm_bias: float32 [512], replicated, may hold values from -4 to 4
- hidden_grad: bfloat16 [32, 1024, 16, 128], P('vtx', 'snap'), may hold values from -6 to 6
Outputs:
- hidden_states: bfloat16 [32, 1024, 16, 128], P('vtx', 'snap')
- grad_gcn_weight: float32 [128, 128], replicated
- grad_gcn_bias: float32 [128], replicated
- grad_input_weight: float32 [128, 512], replicated
- grad_recur_weight: float32 [128, 512], replicated
- grad_lstm_bias: float32 [512], replicated
The draws below stay inside these ranges and needn't reach their ends.
Inputs may be any that keep to these rules, and one draw needn't show every extreme that they name: `tile_cols`: within one snapshot, the 16 slots of one row block name distinct column blocks, and all slots, live or not, of the row blocks j * 8 to (j + 1) * 8 - 1 together name at most one block of each group of 8 consecutive blocks.
All inputs are finite; a program needn't handle non-finite values.
Results may differ from the reference program's by a relative error of at most 0.0085.
Values may be sent and summed in bfloat16 or wider, within the bound.
No kernel may reach another device: no remote copies, remote signals or barrier semaphores. Data moves between devices by JAX's collectives and lax.ppermute only.
A program may use at most 128 MiB of HBM per device.

```python
import jax
import jax.numpy as jnp
from jax import lax

F = 128
HID = 128
TILE = 128
VB_DEV = 8
MAXB = 16
NBLK = 256
V = 32768
SNAPS = 16
N_VTX = 32


def draw_tile_cols(key, part):
    key_order = jax.random.fold_in(key, 11)
    key_pick = jax.random.fold_in(key, 12)
    scores = jax.random.randint(key_order, (SNAPS, NBLK, N_VTX), 0, 2 ** 20) * N_VTX + jnp.arange(N_VTX, dtype=jnp.int32)
    peer_order = jnp.argsort(scores, axis=2)[:, :, :MAXB].astype(jnp.int32)
    picks = jax.random.randint(key_pick, (SNAPS, N_VTX, N_VTX), 0, VB_DEV)
    holder = jnp.arange(NBLK, dtype=jnp.int32) // VB_DEV
    picked_rows = picks[:, holder, :]
    chosen = jnp.take_along_axis(picked_rows, peer_order, axis=2)
    return (peer_order * VB_DEV + chosen).astype(jnp.int32)


def draw_tile_count(key, part):
    key_level = jax.random.fold_in(key, 21)
    key_count = jax.random.fold_in(key, 22)
    key_spot = jax.random.fold_in(key, 23)
    levels = jax.random.randint(key_level, (SNAPS, N_VTX), MAXB // 2, MAXB + 1)
    holder = jnp.arange(NBLK, dtype=jnp.int32) // VB_DEV
    ceiling = levels[:, holder]
    counts = jax.random.randint(key_count, (SNAPS, NBLK), 0, 2 ** 20) % ceiling + 1
    spot = jax.random.randint(key_spot, (), 0, SNAPS * NBLK)
    counts = counts.reshape(-1).at[spot].set(MAXB).reshape(SNAPS, NBLK)
    return counts.astype(jnp.int32)


def steps_of(rng, extent, cuts, least, top_value):
    loudness, own = 1.0, jax.random.fold_in(rng, 6)
    for axis_at, blocks in cuts:
        heights = jnp.exp(jax.random.uniform(jax.random.fold_in(own, axis_at), (blocks,), jnp.float32, least / len(cuts), top_value / len(cuts)))
        loudness = loudness * jnp.repeat(heights, extent[axis_at] // blocks).reshape([-1 if axis == axis_at else 1 for axis in range(len(extent))])
    return loudness


def bell_draw(own_key, shape, scale, reach, split=(), held_as=jnp.bfloat16):
    values = jax.random.normal(own_key, shape, jnp.float32) * scale
    if len(split) > 0:
        values = steps_of(own_key, shape, split, -0.22, 0.18) * values
    return jnp.clip(values, min=-reach, max=reach).astype(held_as)


def setup_inputs(seed: int = 0) -> dict:
    seeds = jax.random.split(jax.random.key(seed), 11)
    features = bell_draw(seeds[0], (SNAPS, V, F), 1.0, 6.0, ((0, 8), (1, 32)))
    tile_vals = bell_draw(seeds[1], (SNAPS, NBLK, MAXB, TILE, TILE), (TILE * 4) ** -0.5, 0.25, ((0, 8), (1, 32)))
    tile_cols = draw_tile_cols(jax.random.fold_in(seeds[10], 71), 0)
    tile_count = draw_tile_count(jax.random.fold_in(seeds[10], 71), 0)
    gcn_weight = bell_draw(seeds[4], (F, F), F ** -0.5, 0.5)
    gcn_bias = bell_draw(seeds[5], (F,), 0.5, 3.0, (), jnp.float32)
    input_weight = bell_draw(seeds[6], (F, 4 * HID), F ** -0.5, 0.5)
    recur_weight = bell_draw(seeds[7], (HID, 4 * HID), HID ** -0.5, 0.5)
    lstm_bias = bell_draw(seeds[8], (4 * HID,), 1.0, 4.0, (), jnp.float32)
    hidden_grad = bell_draw(seeds[9], (N_VTX, VB_DEV * TILE, SNAPS, HID), 1.0, 6.0, ((0, 32), (1, 8)))
    return {"features": features, "tile_vals": tile_vals, "tile_cols": tile_cols, "tile_count": tile_count, "gcn_weight": gcn_weight, "gcn_bias": gcn_bias, "input_weight": input_weight, "recur_weight": recur_weight, "lstm_bias": lstm_bias, "hidden_grad": hidden_grad}


def aggregate_snapshot(packed):
    feats, tiles, cols, counts = packed
    blocks = feats.reshape(NBLK, TILE, F)
    live_mask = jnp.arange(MAXB, dtype=jnp.int32)[None, :] < counts[:, None]
    fetched = jnp.where(live_mask[:, :, None, None], blocks[cols], 0).astype(jnp.float32)
    summed = jnp.einsum('rmij,rmjf->rif', tiles.astype(jnp.float32), fetched)
    return summed.astype(jnp.bfloat16).reshape(NBLK * TILE, F)


def reference(features, tile_vals, tile_cols, tile_count, gcn_weight, gcn_bias, input_weight, recur_weight, lstm_bias, hidden_grad):
    aggregated = lax.map(aggregate_snapshot, (features, tile_vals, tile_cols, tile_count))
    flat_agg = aggregated.reshape(SNAPS * V, F)
    pre_act = jnp.dot(flat_agg, gcn_weight, preferred_element_type=jnp.float32) + gcn_bias
    layer_out = jax.nn.silu(pre_act).astype(jnp.bfloat16)
    layer_seq = layer_out.reshape(SNAPS, V, F)

    def advance(carried, layer_step):
        cell_state, last_out = carried
        input_gates = jnp.dot(layer_step, input_weight, preferred_element_type=jnp.float32) + lstm_bias
        pre_gates = input_gates + jnp.dot(last_out, recur_weight, preferred_element_type=jnp.float32)
        gate_in = jax.nn.sigmoid(pre_gates[:, :HID])
        gate_keep = jax.nn.sigmoid(pre_gates[:, HID:2 * HID])
        gate_new = jnp.tanh(pre_gates[:, 2 * HID:3 * HID])
        gate_out = jax.nn.sigmoid(pre_gates[:, 3 * HID:])
        cell_state = gate_keep * cell_state + gate_in * gate_new
        new_out = (gate_out * jnp.tanh(cell_state)).astype(jnp.bfloat16)
        return (cell_state, new_out), (pre_gates, cell_state, new_out)

    start = (jnp.zeros((V, HID), jnp.float32), jnp.zeros((V, HID), jnp.bfloat16))
    _, (all_pre, all_cells, all_outs) = lax.scan(advance, start, layer_seq)
    prev_cells = jnp.concatenate([jnp.zeros((1, V, HID), jnp.float32), all_cells[:-1]], axis=0)
    prev_outs = jnp.concatenate([jnp.zeros((1, V, HID), jnp.bfloat16), all_outs[:-1]], axis=0)
    grad_outs = hidden_grad.reshape(V, SNAPS, HID).transpose(1, 0, 2).astype(jnp.float32)

    def retreat(carried, step_items):
        grad_cell, grad_back = carried
        pre_gates, cell_state, prev_cell, grad_out = step_items
        gate_in = jax.nn.sigmoid(pre_gates[:, :HID])
        gate_keep = jax.nn.sigmoid(pre_gates[:, HID:2 * HID])
        gate_new = jnp.tanh(pre_gates[:, 2 * HID:3 * HID])
        gate_out = jax.nn.sigmoid(pre_gates[:, 3 * HID:])
        squash = jnp.tanh(cell_state)
        grad_total = grad_out + grad_back
        grad_cell = grad_cell + grad_total * gate_out * (1.0 - squash * squash)
        grad_gates = jnp.concatenate([
            grad_cell * gate_new * gate_in * (1.0 - gate_in),
            grad_cell * prev_cell * gate_keep * (1.0 - gate_keep),
            grad_cell * gate_in * (1.0 - gate_new * gate_new),
            grad_total * squash * gate_out * (1.0 - gate_out)], axis=1).astype(jnp.bfloat16)
        grad_back = jnp.einsum('rg,hg->rh', grad_gates, recur_weight, preferred_element_type=jnp.float32)
        return (grad_cell * gate_keep, grad_back), grad_gates

    _, all_grad_gates = lax.scan(retreat, (jnp.zeros((V, HID), jnp.float32), jnp.zeros((V, HID), jnp.float32)), (all_pre, all_cells, prev_cells, grad_outs), reverse=True)
    flat_gates = all_grad_gates.reshape(SNAPS * V, 4 * HID)
    grad_input = jnp.einsum('rf,rg->fg', layer_out, flat_gates, preferred_element_type=jnp.float32)
    grad_recur = jnp.einsum('rh,rg->hg', prev_outs.reshape(SNAPS * V, HID), flat_gates, preferred_element_type=jnp.float32)
    grad_bias = jnp.sum(flat_gates.astype(jnp.float32), axis=0)
    grad_layer = jnp.einsum('rg,fg->rf', flat_gates, input_weight, preferred_element_type=jnp.float32).astype(jnp.bfloat16)
    squeeze = jax.nn.sigmoid(pre_act)
    grad_pre = (grad_layer.astype(jnp.float32) * squeeze * (1.0 + pre_act * (1.0 - squeeze))).astype(jnp.bfloat16)
    grad_gcn = jnp.einsum('rf,rg->fg', flat_agg, grad_pre, preferred_element_type=jnp.float32)
    grad_gbias = jnp.sum(grad_pre.astype(jnp.float32), axis=0)
    hidden_states = all_outs.transpose(1, 0, 2).reshape(N_VTX, V // N_VTX, SNAPS, HID)
    return (hidden_states, grad_gcn, grad_gbias, grad_input, grad_recur, grad_bias)
```

```python
import jax
import jax.numpy as jnp
from jax import lax
from jax.experimental import pallas as pl
from jax.experimental.pallas import tpu as pltpu
from jax.sharding import PartitionSpec as P

BF16 = jnp.bfloat16
F32 = jnp.float32
MIB = 1024 * 1024


def sigmoid(value):
    return 0.5 * jnp.tanh(0.5 * value) + 0.5


def pack_blocks(want_ref, feat_ref, send_ref, sems):
    peers, steps = send_ref.shape[:2]
    per_peer = feat_ref.shape[1]
    copies = []
    for peer in range(peers):
        for step in range(steps):
            pick = jnp.clip(want_ref[peer, step], 0, per_peer - 1)
            copy = pltpu.make_async_copy(
                feat_ref.at[step, pick], send_ref.at[peer, step], sems.at[peer, step]
            )
            copy.start()
            copies.append(copy)
    for copy in copies:
        copy.wait()


def aggregate(cols_ref, count_ref, recv_ref, tile_ref, out_ref, *, per_peer, group):
    step, block = pl.program_id(0), pl.program_id(1)
    peers = recv_ref.shape[0]
    slots, size, width = tile_ref.shape[2], tile_ref.shape[4], recv_ref.shape[3]
    live = count_ref[step, block]

    def add_group(at, total):
        tiles, blocks = [], []
        for inner in range(group):
            slot = at * group + inner
            peer = jnp.clip(cols_ref[step, block, slot] // per_peer, 0, peers - 1)
            held = recv_ref[peer, step].astype(F32)
            tiles.append(tile_ref[0, 0, slot])
            blocks.append(jnp.where(slot < live, held, 0.0).astype(BF16))
        return total + jnp.dot(
            jnp.concatenate(tiles, axis=1),
            jnp.concatenate(blocks, axis=0),
            preferred_element_type=F32,
        )

    groups = jnp.clip((live + group - 1) // group, 0, slots // group)
    total = lax.fori_loop(0, groups, add_group, jnp.zeros((size, width), F32))
    out_ref[0, 0] = total.astype(BF16)


def recur(
    agg_ref,
    hgrad_ref,
    gcn_w_ref,
    gcn_b_ref,
    w_ref,
    bias_ref,
    w_back_ref,
    out_ref,
    grads_ref,
    layer_s,
    slope_s,
    gates_s,
    cell_s,
    squash_s,
    hprev_s,
    dgates_s,
    dpre_s,
):
    steps, rows, width = agg_ref.shape
    hid = width

    def layer(t, _):
        pre = jnp.dot(agg_ref[t], gcn_w_ref[...], preferred_element_type=F32) + gcn_b_ref[...]
        squeeze = sigmoid(pre)
        layer_s[t] = (pre * squeeze).astype(BF16)
        slope_s[t] = squeeze * (1.0 + pre * (1.0 - squeeze))
        return 0

    lax.fori_loop(0, steps, layer, 0)

    hprev_s[0] = jnp.zeros((rows, hid), BF16)
    cell_s[0] = jnp.zeros((rows, hid), F32)

    def advance(t, _):
        both = jnp.concatenate([layer_s[t], hprev_s[t]], axis=1)
        pre = jnp.dot(both, w_ref[...], preferred_element_type=F32) + bias_ref[...]
        gate_in = sigmoid(pre[:, :hid])
        gate_keep = sigmoid(pre[:, hid : 2 * hid])
        gate_new = jnp.tanh(pre[:, 2 * hid : 3 * hid])
        gate_out = sigmoid(pre[:, 3 * hid :])
        cell = gate_keep * cell_s[t] + gate_in * gate_new
        squash = jnp.tanh(cell)
        out = (gate_out * squash).astype(BF16)
        gates_s[t, :, :hid] = gate_in
        gates_s[t, :, hid : 2 * hid] = gate_keep
        gates_s[t, :, 2 * hid : 3 * hid] = gate_new
        gates_s[t, :, 3 * hid :] = gate_out
        cell_s[t + 1] = cell
        squash_s[t] = squash
        hprev_s[t + 1] = out
        out_ref[t] = out
        return 0

    lax.fori_loop(0, steps, advance, 0)

    def retreat(k, carried):
        grad_cell, grad_back = carried
        t = steps - 1 - k
        gate_in = gates_s[t, :, :hid]
        gate_keep = gates_s[t, :, hid : 2 * hid]
        gate_new = gates_s[t, :, 2 * hid : 3 * hid]
        gate_out = gates_s[t, :, 3 * hid :]
        squash = squash_s[t]
        grad_total = hgrad_ref[t].astype(F32) + grad_back
        grad_cell = grad_cell + grad_total * gate_out * (1.0 - squash * squash)
        dgates = jnp.concatenate(
            [
                (grad_cell * gate_new * gate_in * (1.0 - gate_in)).astype(BF16),
                (grad_cell * cell_s[t] * gate_keep * (1.0 - gate_keep)).astype(BF16),
                (grad_cell * gate_in * (1.0 - gate_new * gate_new)).astype(BF16),
                (grad_total * squash * gate_out * (1.0 - gate_out)).astype(BF16),
            ],
            axis=1,
        )
        dgates_s[t] = dgates
        back = jnp.dot(dgates, w_back_ref[...], preferred_element_type=F32)
        grad_layer = back[:, :width].astype(BF16).astype(F32)
        dpre_s[t] = (grad_layer * slope_s[t]).astype(BF16)
        return grad_cell * gate_keep, back[:, width:]

    zero = jnp.zeros((rows, hid), F32)
    lax.fori_loop(0, steps, retreat, (zero, zero))

    flat_dgates = dgates_s[...].reshape(steps * rows, 4 * hid)
    flat_dpre = dpre_s[...].reshape(steps * rows, width)

    def over_rows(left, right):
        return lax.dot_general(
            left, right, (((0,), (0,)), ((), ())), preferred_element_type=F32
        )

    ones = jnp.ones((8, steps * rows), BF16)
    grads_ref[:width, : 4 * hid] = over_rows(
        layer_s[...].reshape(steps * rows, width), flat_dgates
    )
    grads_ref[width:, : 4 * hid] = over_rows(
        hprev_s[:steps].reshape(steps * rows, hid), flat_dgates
    )
    grads_ref[:width, 4 * hid :] = over_rows(
        agg_ref[...].reshape(steps * rows, width), flat_dpre
    )
    grads_ref[width:, 4 * hid :] = jnp.zeros((hid, width), F32)
    grad_bias = jnp.dot(ones, flat_dgates, preferred_element_type=F32)
    grad_gbias = jnp.dot(ones, flat_dpre, preferred_element_type=F32)
    for k in range(4):
        grads_ref[width + k : width + k + 1, 4 * hid :] = grad_bias[:1, k * hid : (k + 1) * hid]
    grads_ref[width + 4 : width + 5, 4 * hid :] = grad_gbias[:1]


def on_device(
    features,
    tile_vals,
    tile_cols,
    tile_count,
    gcn_weight,
    gcn_bias,
    input_weight,
    recur_weight,
    lstm_bias,
    hidden_grad,
):
    steps_dev, local_verts, width = features.shape
    blocks, slots, size = tile_vals.shape[1:4]
    hid = recur_weight.shape[0]
    n_vtx, n_snap = lax.axis_size("vtx"), lax.axis_size("snap")
    steps, rows = steps_dev * n_snap, local_verts // n_snap
    smem = pl.BlockSpec(memory_space=pltpu.SMEM)
    vmem = pl.BlockSpec(memory_space=pltpu.VMEM)

    with jax.named_scope("requests"):
        flat_cols = tile_cols.reshape(steps_dev, blocks * slots)
        peer_iota = lax.broadcasted_iota(jnp.int32, (n_vtx, steps_dev, blocks * slots), 0)
        named = (flat_cols // blocks)[None] == peer_iota
        need = jnp.max(jnp.where(named, (flat_cols % blocks)[None], 0), axis=2)
        need = jnp.pad(need, ((0, 0), (0, 128 - steps_dev)))
        want = lax.all_to_all(need, "vtx", 0, 0, tiled=True)

    with jax.named_scope("feature_blocks"):
        send = pl.pallas_call(
            pack_blocks,
            out_shape=jax.ShapeDtypeStruct((n_vtx, steps_dev, size, width), BF16),
            in_specs=[smem, vmem],
            out_specs=pl.BlockSpec(memory_space=pl.ANY),
            scratch_shapes=[pltpu.SemaphoreType.DMA((n_vtx, steps_dev))],
            name="pack_blocks",
        )(want, features.reshape(steps_dev, blocks, size, width))
        recv = lax.all_to_all(send, "vtx", 0, 0, tiled=True)

    with jax.named_scope("aggregate"):
        aggregated = pl.pallas_call(
            lambda *refs: aggregate(*refs, per_peer=blocks, group=4),
            out_shape=jax.ShapeDtypeStruct((blocks, steps_dev, size, width), BF16),
            grid=(steps_dev, blocks),
            in_specs=[
                smem,
                smem,
                vmem,
                pl.BlockSpec((1, 1, slots, size, size), lambda s, r: (s, r, 0, 0, 0)),
            ],
            out_specs=pl.BlockSpec((1, 1, size, width), lambda s, r: (r, s, 0, 0)),
            name="aggregate",
        )(tile_cols, tile_count, recv, tile_vals)

    with jax.named_scope("to_vertices"):
        by_step = lax.all_to_all(
            aggregated.reshape(n_snap, steps_dev, rows, width), "snap", 0, 0, tiled=True
        ).reshape(steps, rows, width)

    with jax.named_scope("recurrence"):
        outs, grads = pl.pallas_call(
            recur,
            out_shape=(
                jax.ShapeDtypeStruct((steps, rows, hid), BF16),
                jax.ShapeDtypeStruct((width + hid, 4 * hid + width), F32),
            ),
            in_specs=[vmem] * 7,
            out_specs=(vmem, vmem),
            scratch_shapes=[
                pltpu.VMEM((steps, rows, width), BF16),
                pltpu.VMEM((steps, rows, width), F32),
                pltpu.VMEM((steps, rows, 4 * hid), F32),
                pltpu.VMEM((steps + 1, rows, hid), F32),
                pltpu.VMEM((steps, rows, hid), F32),
                pltpu.VMEM((steps + 1, rows, hid), BF16),
                pltpu.VMEM((steps, rows, 4 * hid), BF16),
                pltpu.VMEM((steps, rows, width), BF16),
            ],
            compiler_params=pltpu.CompilerParams(vmem_limit_bytes=40 * MIB),
            name="recurrence",
        )(
            by_step,
            jnp.transpose(hidden_grad[0], (1, 0, 2)),
            gcn_weight,
            gcn_bias[None],
            jnp.concatenate([input_weight, recur_weight], axis=0),
            lstm_bias[None],
            jnp.concatenate([input_weight.T, recur_weight.T], axis=1),
        )

    with jax.named_scope("gradient_sums"):
        lanes = grads.shape[1]
        part = lax.all_to_all(grads.reshape(n_snap, n_vtx, lanes), "snap", 0, 0, tiled=True)
        part = lax.all_to_all(jnp.sum(part, axis=0), "vtx", 0, 0, tiled=True)
        part = jnp.broadcast_to(jnp.sum(part, axis=0, keepdims=True), (n_vtx, lanes))
        part = lax.all_to_all(part, "vtx", 0, 0, tiled=True)
        part = jnp.broadcast_to(part[None], (n_snap, n_vtx, lanes))
        total = lax.all_to_all(part, "snap", 0, 0, tiled=True).reshape(n_snap * n_vtx, lanes)

    hidden_states = jnp.transpose(outs, (1, 0, 2))[None]
    return (
        hidden_states,
        total[:width, 4 * hid :],
        total[width + 4, 4 * hid :],
        total[:width, : 4 * hid],
        total[width:, : 4 * hid],
        total[width : width + 4, 4 * hid :].reshape(4 * hid),
    )


def solution(mesh):
    return jax.shard_map(
        on_device,
        mesh=mesh,
        in_specs=(
            P("snap", "vtx", None),
            P("snap", "vtx", None, None, None),
            P("snap", "vtx", None),
            P("snap", "vtx"),
            P(),
            P(),
            P(),
            P(),
            P(),
            P("vtx", "snap", None, None),
        ),
        out_specs=(P("vtx", "snap", None, None), P(), P(), P(), P(), P()),
        check_vma=False,
    )
```

```python
import functools

import jax
import jax.numpy as jnp
from jax import lax
from jax.experimental import pallas as pl
from jax.experimental.pallas import tpu as pltpu
from jax.sharding import Mesh
from jax.sharding import PartitionSpec as P

BF16 = jnp.bfloat16
F32 = jnp.float32
MIB = 1024 * 1024
LANES = 128
VTX, SNAP = ("z", "x"), ("y", "core")
SCATTER, ROUND = ("y", "x"), ("core", "z")


def sigmoid(value):
    return 0.5 * jnp.tanh(0.5 * value) + 0.5


def find_requests(cols_ref, feat_ref, need_ref, held_ref, sem, *, per_peer):
    copy = pltpu.make_async_copy(feat_ref, held_ref, sem)
    copy.start()
    steps, blocks, slots = cols_ref.shape
    peers = need_ref.shape[0]
    peer_iota = lax.broadcasted_iota(jnp.int32, (peers, slots), 0)
    lane = lax.broadcasted_iota(jnp.int32, need_ref.shape, 1)
    need = jnp.zeros(need_ref.shape, jnp.int32)
    for step in range(steps):
        found = jnp.zeros((peers, slots), jnp.int32)
        for block in range(blocks):
            cols = jnp.broadcast_to(cols_ref[step, block : block + 1, :], (peers, slots))
            inner = cols - peer_iota * per_peer
            found = jnp.maximum(found, jnp.where(inner < per_peer, inner, 0))
        need = jnp.where(lane == step, jnp.max(found, axis=1, keepdims=True), need)
    need_ref[...] = need
    copy.wait()


def pack_blocks(want_ref, feat_ref, send_ref):
    peers, steps = send_ref.shape[:2]
    per_peer = feat_ref.shape[1]

    def fill(peer, _):
        for step in range(steps):
            pick = jnp.clip(want_ref[peer, step], 0, per_peer - 1)
            send_ref[peer, step] = feat_ref[step, pick]
        return 0

    lax.fori_loop(0, peers, fill, 0, unroll=4)


def aggregate(cols_ref, count_ref, recv_ref, tile_ref, out_ref, held_tiles, sems, *, per_peer):
    steps, blocks, slots, size = tile_ref.shape[:4]
    peers, width = recv_ref.shape[0], recv_ref.shape[3]

    def fetch(step, block):
        return pltpu.make_async_copy(
            tile_ref.at[step, block], held_tiles.at[step, block], sems.at[step, block]
        )

    for block in range(blocks):
        for step in range(steps):
            fetch(step, block).start()

    def one_block(block, _):
        for step in range(steps):
            fetch(step, block).wait()
        for step in range(steps):
            live = count_ref[step, block]
            total = jnp.zeros((size, width), F32)
            for slot in range(0, slots, 2):
                tiles, held = [], []
                for at in (slot, slot + 1):
                    peer = jnp.clip(cols_ref[step, block, at] // per_peer, 0, peers - 1)
                    picked = recv_ref[peer, step]
                    tiles.append(held_tiles[step, block, at])
                    held.append(lax.select_n(at < live, jnp.zeros_like(picked), picked))
                total = total + jnp.dot(
                    jnp.concatenate(tiles, axis=1),
                    jnp.concatenate(held, axis=0),
                    preferred_element_type=F32,
                )
            out_ref[block, step] = total.astype(BF16)
        return 0

    lax.fori_loop(0, blocks, one_block, 0)


def recur(
    agg_ref,
    hgrad_ref,
    gcn_w_ref,
    gcn_b_ref,
    w_ref,
    bias_ref,
    w_back_ref,
    out_ref,
    grads_ref,
    layer_s,
    slope_s,
    gates_s,
    cell_s,
    squash_s,
    hprev_s,
    dgates_s,
    dpre_s,
):
    steps, rows, width = agg_ref.shape
    hid = width

    def layer(t, _):
        pre = jnp.dot(agg_ref[t], gcn_w_ref[...], preferred_element_type=F32) + gcn_b_ref[...]
        squeeze = sigmoid(pre)
        layer_s[t] = (pre * squeeze).astype(BF16)
        slope_s[t] = squeeze * (1.0 + pre * (1.0 - squeeze))
        return 0

    lax.fori_loop(0, steps, layer, 0)

    hprev_s[0] = jnp.zeros((rows, hid), BF16)
    cell_s[0] = jnp.zeros((rows, hid), F32)

    def advance(t, _):
        both = jnp.concatenate([layer_s[t], hprev_s[t]], axis=1)
        pre = jnp.dot(both, w_ref[...], preferred_element_type=F32) + bias_ref[...]
        gate_in = sigmoid(pre[:, :hid])
        gate_keep = sigmoid(pre[:, hid : 2 * hid])
        gate_new = jnp.tanh(pre[:, 2 * hid : 3 * hid])
        gate_out = sigmoid(pre[:, 3 * hid :])
        cell = gate_keep * cell_s[t] + gate_in * gate_new
        squash = jnp.tanh(cell)
        out = (gate_out * squash).astype(BF16)
        gates_s[t, :, :hid] = gate_in
        gates_s[t, :, hid : 2 * hid] = gate_keep
        gates_s[t, :, 2 * hid : 3 * hid] = gate_new
        gates_s[t, :, 3 * hid :] = gate_out
        cell_s[t + 1] = cell
        squash_s[t] = squash
        hprev_s[t + 1] = out
        out_ref[t] = out
        return 0

    lax.fori_loop(0, steps, advance, 0)

    def retreat(k, carried):
        grad_cell, grad_back = carried
        t = steps - 1 - k
        gate_in = gates_s[t, :, :hid]
        gate_keep = gates_s[t, :, hid : 2 * hid]
        gate_new = gates_s[t, :, 2 * hid : 3 * hid]
        gate_out = gates_s[t, :, 3 * hid :]
        squash = squash_s[t]
        grad_total = hgrad_ref[t].astype(F32) + grad_back
        grad_cell = grad_cell + grad_total * gate_out * (1.0 - squash * squash)
        dgates = jnp.concatenate(
            [
                (grad_cell * gate_new * gate_in * (1.0 - gate_in)).astype(BF16),
                (grad_cell * cell_s[t] * gate_keep * (1.0 - gate_keep)).astype(BF16),
                (grad_cell * gate_in * (1.0 - gate_new * gate_new)).astype(BF16),
                (grad_total * squash * gate_out * (1.0 - gate_out)).astype(BF16),
            ],
            axis=1,
        )
        dgates_s[t] = dgates
        back = jnp.dot(dgates, w_back_ref[...], preferred_element_type=F32)
        grad_layer = back[:, :width].astype(BF16).astype(F32)
        dpre_s[t] = (grad_layer * slope_s[t]).astype(BF16)
        return grad_cell * gate_keep, back[:, width:]

    zero = jnp.zeros((rows, hid), F32)
    lax.fori_loop(0, steps, retreat, (zero, zero))

    flat_dgates = dgates_s[...].reshape(steps * rows, 4 * hid)
    flat_dpre = dpre_s[...].reshape(steps * rows, width)

    def over_rows(left, right):
        return lax.dot_general(
            left, right, (((0,), (0,)), ((), ())), preferred_element_type=F32
        )

    def put(at, value):
        height = value.shape[0]
        for k in range(value.shape[1] // LANES):
            grads_ref[pl.ds(at + k * height, height), :] = value[
                :, k * LANES : (k + 1) * LANES
            ].astype(BF16)
        return at + value.shape[1] // LANES * height

    ones = jnp.ones((8, steps * rows), BF16)
    at = put(0, over_rows(layer_s[...].reshape(steps * rows, width), flat_dgates))
    at = put(at, over_rows(hprev_s[:steps].reshape(steps * rows, hid), flat_dgates))
    at = put(at, over_rows(agg_ref[...].reshape(steps * rows, width), flat_dpre))
    at = put(at, jnp.dot(ones, flat_dgates, preferred_element_type=F32))
    at = put(at, jnp.dot(ones, flat_dpre, preferred_element_type=F32))
    grads_ref[pl.ds(at, grads_ref.shape[0] - at), :] = jnp.zeros(
        (grads_ref.shape[0] - at, LANES), BF16
    )


def sum_parts(part_ref, out_ref):
    total = jnp.sum(part_ref[...].astype(F32), axis=0)
    out_ref[...] = jnp.broadcast_to(total.astype(out_ref.dtype)[None], out_ref.shape)


def unpack(total_ref, *out_refs):
    at = 0
    for out_ref in out_refs:
        height, columns = out_ref.shape
        taken = max(height, 8)
        for k in range(columns // LANES):
            out_ref[:, k * LANES : (k + 1) * LANES] = total_ref[pl.ds(at, taken), :].astype(F32)[
                :height
            ]
            at += taken


def on_device(
    features,
    tile_vals,
    tile_cols,
    tile_count,
    gcn_weight,
    gcn_bias,
    input_weight,
    recur_weight,
    lstm_bias,
    hidden_grad,
):
    steps_dev, local_verts, width = features.shape
    blocks, slots, size = tile_vals.shape[1:4]
    hid = recur_weight.shape[0]
    n_vtx, n_snap = lax.axis_size(VTX), lax.axis_size(SNAP)
    steps, rows = steps_dev * n_snap, local_verts // n_snap
    n_scatter, n_round = lax.axis_size(SCATTER), lax.axis_size(ROUND)
    held_rows = (2 * 4 * hid + width) * width // LANES + 8 * (4 * hid + width) // LANES
    share = -(-held_rows // (8 * n_scatter)) * 8
    grad_rows = n_scatter * share
    smem = pl.BlockSpec(memory_space=pltpu.SMEM)
    vmem = pl.BlockSpec(memory_space=pltpu.VMEM)
    hbm = pl.BlockSpec(memory_space=pltpu.HBM)

    with jax.named_scope("requests"):
        need, held_features = pl.pallas_call(
            functools.partial(find_requests, per_peer=blocks),
            out_shape=(
                jax.ShapeDtypeStruct((n_vtx, LANES), jnp.int32),
                jax.ShapeDtypeStruct((steps_dev, blocks, size, width), BF16),
            ),
            in_specs=[vmem, hbm],
            out_specs=(vmem, vmem),
            scratch_shapes=[pltpu.SemaphoreType.DMA],
            compiler_params=pltpu.CompilerParams(vmem_limit_bytes=8 * MIB),
            name="find_requests",
        )(tile_cols, features.reshape(steps_dev, blocks, size, width))
        want = lax.all_to_all(need, VTX, 0, 0, tiled=True)

    with jax.named_scope("feature_blocks"):
        send = pl.pallas_call(
            pack_blocks,
            out_shape=jax.ShapeDtypeStruct((n_vtx, steps_dev, size, width), BF16),
            in_specs=[smem, vmem],
            out_specs=vmem,
            compiler_params=pltpu.CompilerParams(vmem_limit_bytes=8 * MIB),
            name="pack_blocks",
        )(want, held_features)
        recv = lax.all_to_all(send, VTX, 0, 0, tiled=True)

    with jax.named_scope("aggregate"):
        aggregated = pl.pallas_call(
            functools.partial(aggregate, per_peer=blocks),
            out_shape=jax.ShapeDtypeStruct((blocks, steps_dev, size, width), BF16),
            in_specs=[smem, smem, vmem, hbm],
            out_specs=vmem,
            scratch_shapes=[
                pltpu.VMEM(tile_vals.shape, BF16),
                pltpu.SemaphoreType.DMA((steps_dev, blocks)),
            ],
            compiler_params=pltpu.CompilerParams(vmem_limit_bytes=50 * MIB),
            name="aggregate",
        )(tile_cols, tile_count, recv, tile_vals)

    with jax.named_scope("to_vertices"):
        by_step = lax.all_to_all(
            aggregated.reshape(n_snap, steps_dev, rows, width), SNAP, 0, 0, tiled=True
        ).reshape(steps, rows, width)

    with jax.named_scope("recurrence"):
        outs, grads = pl.pallas_call(
            recur,
            out_shape=(
                jax.ShapeDtypeStruct((steps, rows, hid), BF16),
                jax.ShapeDtypeStruct((grad_rows, LANES), BF16),
            ),
            in_specs=[vmem] * 7,
            out_specs=(vmem, vmem),
            scratch_shapes=[
                pltpu.VMEM((steps, rows, width), BF16),
                pltpu.VMEM((steps, rows, width), F32),
                pltpu.VMEM((steps, rows, 4 * hid), F32),
                pltpu.VMEM((steps + 1, rows, hid), F32),
                pltpu.VMEM((steps, rows, hid), F32),
                pltpu.VMEM((steps + 1, rows, hid), BF16),
                pltpu.VMEM((steps, rows, 4 * hid), BF16),
                pltpu.VMEM((steps, rows, width), BF16),
            ],
            compiler_params=pltpu.CompilerParams(vmem_limit_bytes=40 * MIB),
            name="recurrence",
        )(
            by_step,
            jnp.transpose(hidden_grad[0], (1, 0, 2)),
            gcn_weight,
            gcn_bias[None],
            jnp.concatenate([input_weight, recur_weight], axis=0),
            lstm_bias[None],
            jnp.concatenate([input_weight.T, recur_weight.T], axis=1),
        )

    with jax.named_scope("gradient_sums"):
        part = lax.all_to_all(
            grads.reshape(n_scatter, share, LANES), SCATTER, 0, 0, tiled=True
        )
        part = pl.pallas_call(
            sum_parts,
            out_shape=jax.ShapeDtypeStruct((n_round, share, LANES), BF16),
            in_specs=[vmem],
            out_specs=vmem,
            compiler_params=pltpu.CompilerParams(vmem_limit_bytes=8 * MIB),
            name="sum_scattered",
        )(part)
        part = lax.all_to_all(part, ROUND, 0, 0, tiled=True)
        part = pl.pallas_call(
            sum_parts,
            out_shape=jax.ShapeDtypeStruct((n_scatter, share, LANES), BF16),
            in_specs=[vmem],
            out_specs=vmem,
            compiler_params=pltpu.CompilerParams(vmem_limit_bytes=8 * MIB),
            name="sum_round",
        )(part)
        total = lax.all_to_all(part, SCATTER, 0, 0, tiled=True)
        grad_input, grad_recur, grad_gcn, grad_bias, grad_gbias = pl.pallas_call(
            unpack,
            out_shape=tuple(
                jax.ShapeDtypeStruct(shape, F32)
                for shape in (
                    (width, 4 * hid),
                    (hid, 4 * hid),
                    (width, width),
                    (1, 4 * hid),
                    (1, width),
                )
            ),
            in_specs=[vmem],
            out_specs=(vmem,) * 5,
            compiler_params=pltpu.CompilerParams(vmem_limit_bytes=8 * MIB),
            name="unpack",
        )(total.reshape(grad_rows, LANES))

    hidden_states = jnp.transpose(outs, (1, 0, 2))[None]
    return (hidden_states, grad_gcn, grad_gbias[0], grad_input, grad_recur, grad_bias[0])


def solution(mesh):
    fine = Mesh(mesh.devices.reshape(4, 2, 8, 4), ("y", "core", "z", "x"))
    return jax.shard_map(
        on_device,
        mesh=fine,
        in_specs=(
            P(SNAP, VTX, None),
            P(SNAP, VTX, None, None, None),
            P(SNAP, VTX, None),
            P(SNAP, VTX),
            P(),
            P(),
            P(),
            P(),
            P(),
            P(VTX, SNAP, None, None),
        ),
        out_specs=(P(VTX, SNAP, None, None), P(), P(), P(), P(), P()),
        check_vma=False,
    )
```

```python
import functools

import jax
import jax.numpy as jnp
from jax import lax
from jax.experimental import pallas as pl
from jax.experimental.pallas import tpu as pltpu
from jax.sharding import Mesh
from jax.sharding import PartitionSpec as P

BF16 = jnp.bfloat16
F32 = jnp.float32
MIB = 1024 * 1024
LANES = 128
VTX, SNAP = ("z", "x"), ("y", "core")
SCATTER, ROUND = ("y", "x"), ("core", "z")


def sigmoid(value):
    return 0.5 * jnp.tanh(0.5 * value) + 0.5


def find_requests(cols_ref, need_ref, *, per_peer):
    steps, blocks, slots = cols_ref.shape
    peers = need_ref.shape[0]
    peer_iota = lax.broadcasted_iota(jnp.int32, (peers, slots), 0)
    lane = lax.broadcasted_iota(jnp.int32, need_ref.shape, 1)
    need = jnp.zeros(need_ref.shape, jnp.int32)
    for step in range(steps):
        found = jnp.zeros((peers, slots), jnp.int32)
        for block in range(blocks):
            cols = jnp.broadcast_to(cols_ref[step, block : block + 1, :], (peers, slots))
            inner = cols - peer_iota * per_peer
            found = jnp.maximum(found, jnp.where(inner < per_peer, inner, 0))
        need = jnp.where(lane == step, jnp.max(found, axis=1, keepdims=True), need)
    need_ref[...] = need


def stage(from_ref, to_ref, sem):
    copy = pltpu.make_async_copy(from_ref, to_ref, sem)
    copy.start()
    copy.wait()


def staged(value, limit, name):
    return pl.pallas_call(
        stage,
        out_shape=jax.ShapeDtypeStruct(value.shape, value.dtype),
        in_specs=[pl.BlockSpec(memory_space=pltpu.HBM)],
        out_specs=pl.BlockSpec(memory_space=pltpu.VMEM),
        scratch_shapes=[pltpu.SemaphoreType.DMA],
        compiler_params=pltpu.CompilerParams(vmem_limit_bytes=limit),
        cost_estimate=pl.CostEstimate(
            flops=0, bytes_accessed=2 * value.size * value.dtype.itemsize, transcendentals=0
        ),
        name=name,
    )(value)


def pack_blocks(want_ref, feat_ref, send_ref):
    peers, steps = send_ref.shape[:2]
    per_peer = feat_ref.shape[1]

    def fill(peer, _):
        for step in range(steps):
            pick = jnp.clip(want_ref[peer, step], 0, per_peer - 1)
            send_ref[peer, step] = feat_ref[step, pick]
        return 0

    lax.fori_loop(0, peers, fill, 0, unroll=4)


def aggregate(cols_ref, count_ref, recv_ref, tile_ref, out_ref, held_tiles, sems, *, per_peer):
    steps, blocks, slots, size = tile_ref.shape[:4]
    peers, width = recv_ref.shape[0], recv_ref.shape[3]

    def fetch(step, block):
        return pltpu.make_async_copy(
            tile_ref.at[step, block], held_tiles.at[step, block], sems.at[step, block]
        )

    for block in range(blocks):
        for step in range(steps):
            fetch(step, block).start()

    def one_block(block, _):
        for step in range(steps):
            fetch(step, block).wait()
        for step in range(steps):
            live = count_ref[step, block]
            total = jnp.zeros((size, width), F32)
            for slot in range(0, slots, 2):
                tiles, held = [], []
                for at in (slot, slot + 1):
                    peer = jnp.clip(lax.div(cols_ref[step, block, at], per_peer), 0, peers - 1)
                    picked = recv_ref[peer, step]
                    tiles.append(held_tiles[step, block, at])
                    held.append(lax.select_n(at < live, jnp.zeros_like(picked), picked))
                total = total + jnp.dot(
                    jnp.concatenate(tiles, axis=1),
                    jnp.concatenate(held, axis=0),
                    preferred_element_type=F32,
                )
            out_ref[block, step] = total.astype(BF16)
        return 0

    lax.fori_loop(0, blocks, one_block, 0)


def recur(
    agg_ref,
    hgrad_ref,
    gcn_w_ref,
    gcn_b_ref,
    w_ref,
    bias_ref,
    w_back_ref,
    out_ref,
    grads_ref,
    layer_s,
    slope_s,
    gates_s,
    cell_s,
    squash_s,
    hprev_s,
    dgates_s,
    dpre_s,
):
    steps, rows, width = agg_ref.shape
    hid = width

    def layer(t, _):
        pre = jnp.dot(agg_ref[t], gcn_w_ref[...], preferred_element_type=F32) + gcn_b_ref[...]
        squeeze = sigmoid(pre)
        layer_s[t] = (pre * squeeze).astype(BF16)
        slope_s[t] = squeeze * (1.0 + pre * (1.0 - squeeze))
        return 0

    lax.fori_loop(0, steps, layer, 0, unroll=4)

    hprev_s[0] = jnp.zeros((rows, hid), BF16)
    cell_s[0] = jnp.zeros((rows, hid), F32)

    def advance(t, _):
        both = jnp.concatenate([layer_s[t], hprev_s[t]], axis=1)
        pre = jnp.dot(both, w_ref[...], preferred_element_type=F32) + bias_ref[...]
        gate_in = sigmoid(pre[:, :hid])
        gate_keep = sigmoid(pre[:, hid : 2 * hid])
        gate_new = jnp.tanh(pre[:, 2 * hid : 3 * hid])
        gate_out = sigmoid(pre[:, 3 * hid :])
        cell = gate_keep * cell_s[t] + gate_in * gate_new
        squash = jnp.tanh(cell)
        out = (gate_out * squash).astype(BF16)
        gates_s[t, :, :hid] = gate_in
        gates_s[t, :, hid : 2 * hid] = gate_keep
        gates_s[t, :, 2 * hid : 3 * hid] = gate_new
        gates_s[t, :, 3 * hid :] = gate_out
        cell_s[t + 1] = cell
        squash_s[t] = squash
        hprev_s[t + 1] = out
        out_ref[t] = out
        return 0

    lax.fori_loop(0, steps, advance, 0, unroll=4)

    def retreat(k, carried):
        grad_cell, grad_back = carried
        t = steps - 1 - k
        gate_in = gates_s[t, :, :hid]
        gate_keep = gates_s[t, :, hid : 2 * hid]
        gate_new = gates_s[t, :, 2 * hid : 3 * hid]
        gate_out = gates_s[t, :, 3 * hid :]
        squash = squash_s[t]
        grad_total = hgrad_ref[t].astype(F32) + grad_back
        grad_cell = grad_cell + grad_total * gate_out * (1.0 - squash * squash)
        dgates = jnp.concatenate(
            [
                (grad_cell * gate_new * gate_in * (1.0 - gate_in)).astype(BF16),
                (grad_cell * cell_s[t] * gate_keep * (1.0 - gate_keep)).astype(BF16),
                (grad_cell * gate_in * (1.0 - gate_new * gate_new)).astype(BF16),
                (grad_total * squash * gate_out * (1.0 - gate_out)).astype(BF16),
            ],
            axis=1,
        )
        dgates_s[t] = dgates
        back = jnp.dot(dgates, w_back_ref[...], preferred_element_type=F32)
        grad_layer = back[:, :width].astype(BF16).astype(F32)
        dpre_s[t] = (grad_layer * slope_s[t]).astype(BF16)
        return grad_cell * gate_keep, back[:, width:]

    zero = jnp.zeros((rows, hid), F32)
    lax.fori_loop(0, steps, retreat, (zero, zero), unroll=4)

    flat_dgates = dgates_s[...].reshape(steps * rows, 4 * hid)
    flat_dpre = dpre_s[...].reshape(steps * rows, width)

    def over_rows(left, right):
        return lax.dot_general(
            left, right, (((0,), (0,)), ((), ())), preferred_element_type=F32
        )

    def put(at, value):
        height = value.shape[0]
        for k in range(value.shape[1] // LANES):
            grads_ref[pl.ds(at + k * height, height), :] = value[
                :, k * LANES : (k + 1) * LANES
            ].astype(BF16)
        return at + value.shape[1] // LANES * height

    ones = jnp.ones((8, steps * rows), BF16)
    at = put(0, over_rows(layer_s[...].reshape(steps * rows, width), flat_dgates))
    at = put(at, over_rows(hprev_s[:steps].reshape(steps * rows, hid), flat_dgates))
    at = put(at, over_rows(agg_ref[...].reshape(steps * rows, width), flat_dpre))
    at = put(at, jnp.dot(ones, flat_dgates, preferred_element_type=F32))
    at = put(at, jnp.dot(ones, flat_dpre, preferred_element_type=F32))
    grads_ref[pl.ds(at, grads_ref.shape[0] - at), :] = jnp.zeros(
        (grads_ref.shape[0] - at, LANES), BF16
    )


def sum_parts(part_ref, out_ref):
    total = jnp.sum(part_ref[...].astype(F32), axis=0)
    out_ref[...] = jnp.broadcast_to(total.astype(out_ref.dtype)[None], out_ref.shape)


def unpack(total_ref, *out_refs):
    at = 0
    for out_ref in out_refs:
        height, columns = out_ref.shape
        taken = max(height, 8)
        for k in range(columns // LANES):
            out_ref[:, k * LANES : (k + 1) * LANES] = total_ref[pl.ds(at, taken), :].astype(F32)[
                :height
            ]
            at += taken


def on_device(
    features,
    tile_vals,
    tile_cols,
    tile_count,
    gcn_weight,
    gcn_bias,
    input_weight,
    recur_weight,
    lstm_bias,
    hidden_grad,
):
    steps_dev, local_verts, width = features.shape
    blocks, slots, size = tile_vals.shape[1:4]
    hid = recur_weight.shape[0]
    n_vtx, n_snap = lax.axis_size(VTX), lax.axis_size(SNAP)
    steps, rows = steps_dev * n_snap, local_verts // n_snap
    n_scatter, n_round = lax.axis_size(SCATTER), lax.axis_size(ROUND)
    held_rows = (2 * 4 * hid + width) * width // LANES + 8 * (4 * hid + width) // LANES
    share = -(-held_rows // (8 * n_scatter)) * 8
    grad_rows = n_scatter * share
    smem = pl.BlockSpec(memory_space=pltpu.SMEM)
    vmem = pl.BlockSpec(memory_space=pltpu.VMEM)
    hbm = pl.BlockSpec(memory_space=pltpu.HBM)

    with jax.named_scope("requests"):
        need = pl.pallas_call(
            functools.partial(find_requests, per_peer=blocks),
            out_shape=jax.ShapeDtypeStruct((n_vtx, LANES), jnp.int32),
            in_specs=[vmem],
            out_specs=vmem,
            compiler_params=pltpu.CompilerParams(vmem_limit_bytes=8 * MIB),
            name="find_requests",
        )(tile_cols)
        held_features = staged(
            features.reshape(steps_dev, blocks, size, width), 50 * MIB, "stage_features"
        )
        want = lax.all_to_all(need, VTX, 0, 0, tiled=True)

    with jax.named_scope("feature_blocks"):
        send = pl.pallas_call(
            pack_blocks,
            out_shape=jax.ShapeDtypeStruct((n_vtx, steps_dev, size, width), BF16),
            in_specs=[smem, vmem],
            out_specs=vmem,
            compiler_params=pltpu.CompilerParams(vmem_limit_bytes=8 * MIB),
            name="pack_blocks",
        )(want, held_features)
        recv = lax.all_to_all(send, VTX, 0, 0, tiled=True)

    with jax.named_scope("aggregate"):
        aggregated = pl.pallas_call(
            functools.partial(aggregate, per_peer=blocks),
            out_shape=jax.ShapeDtypeStruct((blocks, steps_dev, size, width), BF16),
            in_specs=[smem, smem, vmem, hbm],
            out_specs=vmem,
            scratch_shapes=[
                pltpu.VMEM(tile_vals.shape, BF16),
                pltpu.SemaphoreType.DMA((steps_dev, blocks)),
            ],
            compiler_params=pltpu.CompilerParams(vmem_limit_bytes=50 * MIB),
            name="aggregate",
        )(tile_cols, tile_count, recv, tile_vals)

    with jax.named_scope("to_vertices"):
        by_step = lax.all_to_all(
            aggregated.reshape(n_snap, steps_dev, rows, width), SNAP, 0, 0, tiled=True
        ).reshape(steps, rows, width)

    with jax.named_scope("recurrence"):
        outs, grads = pl.pallas_call(
            recur,
            out_shape=(
                jax.ShapeDtypeStruct((steps, rows, hid), BF16),
                jax.ShapeDtypeStruct((grad_rows, LANES), BF16),
            ),
            in_specs=[vmem] * 7,
            out_specs=(vmem, vmem),
            scratch_shapes=[
                pltpu.VMEM((steps, rows, width), BF16),
                pltpu.VMEM((steps, rows, width), F32),
                pltpu.VMEM((steps, rows, 4 * hid), F32),
                pltpu.VMEM((steps + 1, rows, hid), F32),
                pltpu.VMEM((steps, rows, hid), F32),
                pltpu.VMEM((steps + 1, rows, hid), BF16),
                pltpu.VMEM((steps, rows, 4 * hid), BF16),
                pltpu.VMEM((steps, rows, width), BF16),
            ],
            compiler_params=pltpu.CompilerParams(vmem_limit_bytes=40 * MIB),
            name="recurrence",
        )(
            by_step,
            jnp.transpose(hidden_grad[0], (1, 0, 2)),
            gcn_weight,
            gcn_bias[None],
            jnp.concatenate([input_weight, recur_weight], axis=0),
            lstm_bias[None],
            jnp.concatenate([input_weight.T, recur_weight.T], axis=1),
        )

    with jax.named_scope("gradient_sums"):
        part = lax.all_to_all(
            grads.reshape(n_scatter, share, LANES), SCATTER, 0, 0, tiled=True
        )
        part = pl.pallas_call(
            sum_parts,
            out_shape=jax.ShapeDtypeStruct((n_round, share, LANES), BF16),
            in_specs=[vmem],
            out_specs=vmem,
            compiler_params=pltpu.CompilerParams(vmem_limit_bytes=8 * MIB),
            name="sum_scattered",
        )(part)
        part = lax.all_to_all(part, ROUND, 0, 0, tiled=True)
        part = pl.pallas_call(
            sum_parts,
            out_shape=jax.ShapeDtypeStruct((n_scatter, share, LANES), BF16),
            in_specs=[vmem],
            out_specs=vmem,
            compiler_params=pltpu.CompilerParams(vmem_limit_bytes=8 * MIB),
            name="sum_round",
        )(part)
        total = lax.all_to_all(part, SCATTER, 0, 0, tiled=True)
        grad_input, grad_recur, grad_gcn, grad_bias, grad_gbias = pl.pallas_call(
            unpack,
            out_shape=tuple(
                jax.ShapeDtypeStruct(shape, F32)
                for shape in (
                    (width, 4 * hid),
                    (hid, 4 * hid),
                    (width, width),
                    (1, 4 * hid),
                    (1, width),
                )
            ),
            in_specs=[vmem],
            out_specs=(vmem,) * 5,
            compiler_params=pltpu.CompilerParams(vmem_limit_bytes=8 * MIB),
            name="unpack",
        )(total.reshape(grad_rows, LANES))

    hidden_states = jnp.transpose(outs, (1, 0, 2))[None]
    return (hidden_states, grad_gcn, grad_gbias[0], grad_input, grad_recur, grad_bias[0])


def solution(mesh):
    fine = Mesh(mesh.devices.reshape(4, 2, 8, 4), ("y", "core", "z", "x"))
    return jax.shard_map(
        on_device,
        mesh=fine,
        in_specs=(
            P(SNAP, VTX, None),
            P(SNAP, VTX, None, None, None),
            P(SNAP, VTX, None),
            P(SNAP, VTX),
            P(),
            P(),
            P(),
            P(),
            P(),
            P(VTX, SNAP, None, None),
        ),
        out_specs=(P(VTX, SNAP, None, None), P(), P(), P(), P(), P()),
        check_vma=False,
    )
```

```python
import functools

import jax
import jax.numpy as jnp
from jax import lax
from jax.experimental import pallas as pl
from jax.experimental.pallas import tpu as pltpu
from jax.sharding import Mesh
from jax.sharding import PartitionSpec as P

BF16 = jnp.bfloat16
F32 = jnp.float32
MIB = 1024 * 1024
LANES = 128
VTX, SNAP = ("z", "x"), ("y", "core")
SCATTER, ROUND, PAIR = ("x", "y"), "z", "core"


def sigmoid(value):
    return 0.5 * jnp.tanh(0.5 * value) + 0.5


def find_requests(cols_ref, need_ref, *, per_peer):
    steps, blocks, slots = cols_ref.shape
    peers = need_ref.shape[0]
    peer_iota = lax.broadcasted_iota(jnp.int32, (peers, slots), 0)
    lane = lax.broadcasted_iota(jnp.int32, need_ref.shape, 1)
    need = jnp.zeros(need_ref.shape, jnp.int32)
    for step in range(steps):
        found = jnp.zeros((peers, slots), jnp.int32)
        for block in range(blocks):
            cols = jnp.broadcast_to(cols_ref[step, block : block + 1, :], (peers, slots))
            inner = cols - peer_iota * per_peer
            found = jnp.maximum(found, jnp.where(inner < per_peer, inner, 0))
        need = jnp.where(lane == step, jnp.max(found, axis=1, keepdims=True), need)
    need_ref[...] = need


def stage(from_ref, to_ref, sem):
    copy = pltpu.make_async_copy(from_ref, to_ref, sem)
    copy.start()
    copy.wait()


def staged(value, limit, name):
    return pl.pallas_call(
        stage,
        out_shape=jax.ShapeDtypeStruct(value.shape, value.dtype),
        in_specs=[pl.BlockSpec(memory_space=pltpu.HBM)],
        out_specs=pl.BlockSpec(memory_space=pltpu.VMEM),
        scratch_shapes=[pltpu.SemaphoreType.DMA],
        compiler_params=pltpu.CompilerParams(vmem_limit_bytes=limit),
        cost_estimate=pl.CostEstimate(
            flops=0, bytes_accessed=2 * value.size * value.dtype.itemsize, transcendentals=0
        ),
        name=name,
    )(value)


def pack_blocks(want_ref, feat_ref, send_ref):
    peers, steps = send_ref.shape[:2]
    per_peer = feat_ref.shape[1]

    def fill(peer, _):
        for step in range(steps):
            pick = jnp.clip(want_ref[peer, step], 0, per_peer - 1)
            send_ref[peer, step] = feat_ref[step, pick]
        return 0

    lax.fori_loop(0, peers, fill, 0, unroll=4)


def aggregate(cols_ref, count_ref, recv_ref, tile_ref, out_ref, held_tiles, sems, *, per_peer):
    steps, blocks, slots, size = tile_ref.shape[:4]
    peers, width = recv_ref.shape[0], recv_ref.shape[3]

    def fetch(step, block):
        return pltpu.make_async_copy(
            tile_ref.at[step, block], held_tiles.at[step, block], sems.at[step, block]
        )

    for block in range(blocks):
        for step in range(steps):
            fetch(step, block).start()

    def one_block(block, _):
        for step in range(steps):
            fetch(step, block).wait()
        for step in range(steps):
            live = count_ref[step, block]
            total = jnp.zeros((size, width), F32)
            for slot in range(0, slots, 2):
                tiles, held = [], []
                for at in (slot, slot + 1):
                    peer = jnp.clip(lax.div(cols_ref[step, block, at], per_peer), 0, peers - 1)
                    picked = recv_ref[peer, step]
                    tiles.append(held_tiles[step, block, at])
                    held.append(lax.select_n(at < live, jnp.zeros_like(picked), picked))
                total = total + jnp.dot(
                    jnp.concatenate(tiles, axis=1),
                    jnp.concatenate(held, axis=0),
                    preferred_element_type=F32,
                )
            out_ref[block, step] = total.astype(BF16)
        return 0

    lax.fori_loop(0, blocks, one_block, 0)


def recur(
    core_ref,
    agg_ref,
    hgrad_ref,
    gcn_w_ref,
    gcn_b_ref,
    w_ref,
    bias_ref,
    w_back_ref,
    out_ref,
    keep_ref,
    send_ref,
    layer_s,
    slope_s,
    gates_s,
    cell_s,
    squash_s,
    hprev_s,
    dgates_s,
    dpre_s,
    grads_s,
):
    steps, rows, width = agg_ref.shape
    hid = width

    def layer(t, _):
        pre = jnp.dot(agg_ref[t], gcn_w_ref[...], preferred_element_type=F32) + gcn_b_ref[...]
        squeeze = sigmoid(pre)
        layer_s[t] = (pre * squeeze).astype(BF16)
        slope_s[t] = squeeze * (1.0 + pre * (1.0 - squeeze))
        return 0

    lax.fori_loop(0, steps, layer, 0, unroll=4)

    hprev_s[0] = jnp.zeros((rows, hid), BF16)
    cell_s[0] = jnp.zeros((rows, hid), F32)

    def advance(t, _):
        both = jnp.concatenate([layer_s[t], hprev_s[t]], axis=1)
        pre = jnp.dot(both, w_ref[...], preferred_element_type=F32) + bias_ref[...]
        gate_in = sigmoid(pre[:, :hid])
        gate_keep = sigmoid(pre[:, hid : 2 * hid])
        gate_new = jnp.tanh(pre[:, 2 * hid : 3 * hid])
        gate_out = sigmoid(pre[:, 3 * hid :])
        cell = gate_keep * cell_s[t] + gate_in * gate_new
        squash = jnp.tanh(cell)
        out = (gate_out * squash).astype(BF16)
        gates_s[t, :, :hid] = gate_in
        gates_s[t, :, hid : 2 * hid] = gate_keep
        gates_s[t, :, 2 * hid : 3 * hid] = gate_new
        gates_s[t, :, 3 * hid :] = gate_out
        cell_s[t + 1] = cell
        squash_s[t] = squash
        hprev_s[t + 1] = out
        out_ref[t] = out
        return 0

    lax.fori_loop(0, steps, advance, 0, unroll=4)

    def retreat(k, carried):
        grad_cell, grad_back = carried
        t = steps - 1 - k
        gate_in = gates_s[t, :, :hid]
        gate_keep = gates_s[t, :, hid : 2 * hid]
        gate_new = gates_s[t, :, 2 * hid : 3 * hid]
        gate_out = gates_s[t, :, 3 * hid :]
        squash = squash_s[t]
        grad_total = hgrad_ref[t].astype(F32) + grad_back
        grad_cell = grad_cell + grad_total * gate_out * (1.0 - squash * squash)
        dgates = jnp.concatenate(
            [
                (grad_cell * gate_new * gate_in * (1.0 - gate_in)).astype(BF16),
                (grad_cell * cell_s[t] * gate_keep * (1.0 - gate_keep)).astype(BF16),
                (grad_cell * gate_in * (1.0 - gate_new * gate_new)).astype(BF16),
                (grad_total * squash * gate_out * (1.0 - gate_out)).astype(BF16),
            ],
            axis=1,
        )
        dgates_s[t] = dgates
        back = jnp.dot(dgates, w_back_ref[...], preferred_element_type=F32)
        grad_layer = back[:, :width].astype(BF16).astype(F32)
        dpre_s[t] = (grad_layer * slope_s[t]).astype(BF16)
        return grad_cell * gate_keep, back[:, width:]

    zero = jnp.zeros((rows, hid), F32)
    lax.fori_loop(0, steps, retreat, (zero, zero), unroll=4)

    flat_dgates = dgates_s[...].reshape(steps * rows, 4 * hid)
    flat_dpre = dpre_s[...].reshape(steps * rows, width)

    def over_rows(left, right):
        return lax.dot_general(
            left, right, (((0,), (0,)), ((), ())), preferred_element_type=F32
        )

    def put(at, value):
        height = value.shape[0]
        for k in range(value.shape[1] // LANES):
            grads_s[pl.ds(at + k * height, height), :] = value[:, k * LANES : (k + 1) * LANES]
        return at + value.shape[1] // LANES * height

    ones = jnp.ones((8, steps * rows), BF16)
    at = put(0, over_rows(layer_s[...].reshape(steps * rows, width), flat_dgates))
    at = put(at, over_rows(hprev_s[:steps].reshape(steps * rows, hid), flat_dgates))
    at = put(at, over_rows(agg_ref[...].reshape(steps * rows, width), flat_dpre))
    at = put(at, jnp.dot(ones, flat_dgates, preferred_element_type=F32))
    at = put(at, jnp.dot(ones, flat_dpre, preferred_element_type=F32))
    grads_s[pl.ds(at, grads_s.shape[0] - at), :] = jnp.zeros((grads_s.shape[0] - at, LANES), F32)
    half = keep_ref.shape[0]
    core = core_ref[0]
    keep_ref[...] = grads_s[pl.ds(pl.multiple_of(core * half, 8), half), :]
    send_ref[...] = grads_s[pl.ds(pl.multiple_of((1 - core) * half, 8), half), :]


def sum_pair(left_ref, right_ref, out_ref):
    out_ref[...] = (left_ref[...] + right_ref[...]).astype(out_ref.dtype)


def sum_parts(part_ref, out_ref):
    total = jnp.sum(part_ref[...].astype(F32), axis=0)
    out_ref[...] = jnp.broadcast_to(total.astype(out_ref.dtype)[None], out_ref.shape)


def unpack(core_ref, mine_ref, other_ref, *refs):
    out_refs, total_ref = refs[:-1], refs[-1]
    half = mine_ref.shape[0]
    core = core_ref[0]
    total_ref[pl.ds(pl.multiple_of(core * half, 8), half), :] = mine_ref[...].astype(F32)
    total_ref[pl.ds(pl.multiple_of((1 - core) * half, 8), half), :] = other_ref[...].astype(F32)
    at = 0
    for out_ref in out_refs:
        height, columns = out_ref.shape
        taken = max(height, 8)
        for k in range(columns // LANES):
            out_ref[:, k * LANES : (k + 1) * LANES] = total_ref[pl.ds(at, taken), :][:height]
            at += taken


def on_device(
    features,
    tile_vals,
    tile_cols,
    tile_count,
    gcn_weight,
    gcn_bias,
    input_weight,
    recur_weight,
    lstm_bias,
    hidden_grad,
):
    steps_dev, local_verts, width = features.shape
    blocks, slots, size = tile_vals.shape[1:4]
    hid = recur_weight.shape[0]
    n_vtx, n_snap = lax.axis_size(VTX), lax.axis_size(SNAP)
    steps, rows = steps_dev * n_snap, local_verts // n_snap
    n_scatter, n_round = lax.axis_size(SCATTER), lax.axis_size(ROUND)
    held_rows = (2 * 4 * hid + width) * width // LANES + 8 * (4 * hid + width) // LANES
    share = -(-held_rows // (2 * 8 * n_scatter)) * 8
    half_rows = n_scatter * share
    core = lax.axis_index(PAIR).astype(jnp.int32).reshape(1)
    smem = pl.BlockSpec(memory_space=pltpu.SMEM)
    vmem = pl.BlockSpec(memory_space=pltpu.VMEM)
    hbm = pl.BlockSpec(memory_space=pltpu.HBM)

    with jax.named_scope("requests"):
        need = pl.pallas_call(
            functools.partial(find_requests, per_peer=blocks),
            out_shape=jax.ShapeDtypeStruct((n_vtx, LANES), jnp.int32),
            in_specs=[vmem],
            out_specs=vmem,
            compiler_params=pltpu.CompilerParams(vmem_limit_bytes=8 * MIB),
            name="find_requests",
        )(tile_cols)
        held_features = staged(
            features.reshape(steps_dev, blocks, size, width), 50 * MIB, "stage_features"
        )
        want = lax.all_to_all(need, VTX, 0, 0, tiled=True)

    with jax.named_scope("feature_blocks"):
        send = pl.pallas_call(
            pack_blocks,
            out_shape=jax.ShapeDtypeStruct((n_vtx, steps_dev, size, width), BF16),
            in_specs=[smem, vmem],
            out_specs=vmem,
            compiler_params=pltpu.CompilerParams(vmem_limit_bytes=8 * MIB),
            name="pack_blocks",
        )(want, held_features)
        recv = lax.all_to_all(send, VTX, 0, 0, tiled=True)

    with jax.named_scope("aggregate"):
        aggregated = pl.pallas_call(
            functools.partial(aggregate, per_peer=blocks),
            out_shape=jax.ShapeDtypeStruct((blocks, steps_dev, size, width), BF16),
            in_specs=[smem, smem, vmem, hbm],
            out_specs=vmem,
            scratch_shapes=[
                pltpu.VMEM(tile_vals.shape, BF16),
                pltpu.SemaphoreType.DMA((steps_dev, blocks)),
            ],
            compiler_params=pltpu.CompilerParams(vmem_limit_bytes=50 * MIB),
            name="aggregate",
        )(tile_cols, tile_count, recv, tile_vals)

    with jax.named_scope("to_vertices"):
        by_step = lax.all_to_all(
            aggregated.reshape(n_snap, steps_dev, rows, width), SNAP, 0, 0, tiled=True
        ).reshape(steps, rows, width)

    with jax.named_scope("recurrence"):
        outs, keep, away = pl.pallas_call(
            recur,
            out_shape=(
                jax.ShapeDtypeStruct((steps, rows, hid), BF16),
                jax.ShapeDtypeStruct((half_rows, LANES), F32),
                jax.ShapeDtypeStruct((half_rows, LANES), F32),
            ),
            in_specs=[smem] + [vmem] * 7,
            out_specs=(vmem, vmem, vmem),
            scratch_shapes=[
                pltpu.VMEM((steps, rows, width), BF16),
                pltpu.VMEM((steps, rows, width), F32),
                pltpu.VMEM((steps, rows, 4 * hid), F32),
                pltpu.VMEM((steps + 1, rows, hid), F32),
                pltpu.VMEM((steps, rows, hid), F32),
                pltpu.VMEM((steps + 1, rows, hid), BF16),
                pltpu.VMEM((steps, rows, 4 * hid), BF16),
                pltpu.VMEM((steps, rows, width), BF16),
                pltpu.VMEM((2 * half_rows, LANES), F32),
            ],
            compiler_params=pltpu.CompilerParams(vmem_limit_bytes=40 * MIB),
            name="recurrence",
        )(
            core,
            by_step,
            jnp.transpose(hidden_grad[0], (1, 0, 2)),
            gcn_weight,
            gcn_bias[None],
            jnp.concatenate([input_weight, recur_weight], axis=0),
            lstm_bias[None],
            jnp.concatenate([input_weight.T, recur_weight.T], axis=1),
        )

    with jax.named_scope("gradient_sums"):
        part = pl.pallas_call(
            sum_pair,
            out_shape=jax.ShapeDtypeStruct((half_rows, LANES), BF16),
            in_specs=[vmem, vmem],
            out_specs=vmem,
            compiler_params=pltpu.CompilerParams(vmem_limit_bytes=8 * MIB),
            name="sum_pair",
        )(keep, lax.ppermute(away, PAIR, ((0, 1), (1, 0))))
        part = lax.all_to_all(
            part.reshape(n_scatter, share, LANES), SCATTER, 0, 0, tiled=True
        )
        part = pl.pallas_call(
            sum_parts,
            out_shape=jax.ShapeDtypeStruct((n_round, share, LANES), BF16),
            in_specs=[vmem],
            out_specs=vmem,
            compiler_params=pltpu.CompilerParams(vmem_limit_bytes=8 * MIB),
            name="sum_scattered",
        )(part)
        part = lax.all_to_all(part, ROUND, 0, 0, tiled=True)
        part = pl.pallas_call(
            sum_parts,
            out_shape=jax.ShapeDtypeStruct((n_scatter, share, LANES), BF16),
            in_specs=[vmem],
            out_specs=vmem,
            compiler_params=pltpu.CompilerParams(vmem_limit_bytes=8 * MIB),
            name="sum_round",
        )(part)
        mine = lax.all_to_all(part, SCATTER, 0, 0, tiled=True).reshape(half_rows, LANES)
        other = lax.ppermute(mine, PAIR, ((0, 1), (1, 0)))
        grad_input, grad_recur, grad_gcn, grad_bias, grad_gbias = pl.pallas_call(
            unpack,
            out_shape=tuple(
                jax.ShapeDtypeStruct(shape, F32)
                for shape in (
                    (width, 4 * hid),
                    (hid, 4 * hid),
                    (width, width),
                    (1, 4 * hid),
                    (1, width),
                )
            ),
            in_specs=[smem, vmem, vmem],
            out_specs=(vmem,) * 5,
            scratch_shapes=[pltpu.VMEM((2 * half_rows, LANES), F32)],
            compiler_params=pltpu.CompilerParams(vmem_limit_bytes=8 * MIB),
            name="unpack",
        )(core, mine, other)

    hidden_states = jnp.transpose(outs, (1, 0, 2))[None]
    return (hidden_states, grad_gcn, grad_gbias[0], grad_input, grad_recur, grad_bias[0])


def solution(mesh):
    fine = Mesh(mesh.devices.reshape(4, 2, 8, 4), ("y", "core", "z", "x"))
    return jax.shard_map(
        on_device,
        mesh=fine,
        in_specs=(
            P(SNAP, VTX, None),
            P(SNAP, VTX, None, None, None),
            P(SNAP, VTX, None),
            P(SNAP, VTX),
            P(),
            P(),
            P(),
            P(),
            P(),
            P(VTX, SNAP, None, None),
        ),
        out_specs=(P(VTX, SNAP, None, None), P(), P(), P(), P(), P()),
        check_vma=False,
    )
```

```python
import functools

import jax
import jax.numpy as jnp
from jax import lax
from jax.experimental import pallas as pl
from jax.experimental.pallas import tpu as pltpu
from jax.sharding import Mesh
from jax.sharding import PartitionSpec as P

BF16 = jnp.bfloat16
F32 = jnp.float32
MIB = 1024 * 1024
LANES = 128
VTX, SNAP = ("z", "x"), ("y", "core")
SCATTER, ROUND, PAIR = ("x", "y"), "z", "core"


def sigmoid(value):
    return 0.5 * jnp.tanh(0.5 * value) + 0.5


def find_requests(cols_ref, need_ref, *, per_peer):
    steps, blocks, slots = cols_ref.shape
    peers = need_ref.shape[0]
    peer_iota = lax.broadcasted_iota(jnp.int32, (peers, slots), 0)
    lane = lax.broadcasted_iota(jnp.int32, need_ref.shape, 1)
    need = jnp.zeros(need_ref.shape, jnp.int32)
    for step in range(steps):
        found = jnp.zeros((peers, slots), jnp.int32)
        for block in range(blocks):
            cols = jnp.broadcast_to(cols_ref[step, block : block + 1, :], (peers, slots))
            inner = cols - peer_iota * per_peer
            found = jnp.maximum(found, jnp.where(inner < per_peer, inner, 0))
        need = jnp.where(lane == step, jnp.max(found, axis=1, keepdims=True), need)
    need_ref[...] = need


def stage(from_ref, to_ref, sem):
    copy = pltpu.make_async_copy(from_ref, to_ref, sem)
    copy.start()
    copy.wait()


def staged(value, limit, name):
    return pl.pallas_call(
        stage,
        out_shape=jax.ShapeDtypeStruct(value.shape, value.dtype),
        in_specs=[pl.BlockSpec(memory_space=pltpu.HBM)],
        out_specs=pl.BlockSpec(memory_space=pltpu.VMEM),
        scratch_shapes=[pltpu.SemaphoreType.DMA],
        compiler_params=pltpu.CompilerParams(vmem_limit_bytes=limit),
        cost_estimate=pl.CostEstimate(
            flops=0, bytes_accessed=2 * value.size * value.dtype.itemsize, transcendentals=0
        ),
        name=name,
    )(value)


def pack_blocks(want_ref, feat_ref, tile_ref, send_ref):
    del tile_ref
    peers, steps = send_ref.shape[:2]
    per_peer = feat_ref.shape[1]

    def fill(peer, _):
        for step in range(steps):
            pick = jnp.clip(want_ref[peer, step], 0, per_peer - 1)
            send_ref[peer, step] = feat_ref[step, pick]
        return 0

    lax.fori_loop(0, peers, fill, 0, unroll=4)


def aggregate(cols_ref, count_ref, recv_ref, tile_ref, out_ref, *, per_peer):
    steps, blocks, slots, size = tile_ref.shape[:4]
    peers, width = recv_ref.shape[0], recv_ref.shape[3]

    def one_block(block, _):
        for step in range(steps):
            live = count_ref[step, block]
            total = jnp.zeros((size, width), F32)
            for slot in range(0, slots, 2):
                tiles, held = [], []
                for at in (slot, slot + 1):
                    peer = jnp.clip(lax.div(cols_ref[step, block, at], per_peer), 0, peers - 1)
                    picked = recv_ref[peer, step]
                    tiles.append(tile_ref[step, block, at])
                    held.append(lax.select_n(at < live, jnp.zeros_like(picked), picked))
                total = total + jnp.dot(
                    jnp.concatenate(tiles, axis=1),
                    jnp.concatenate(held, axis=0),
                    preferred_element_type=F32,
                )
            out_ref[block, step] = total.astype(BF16)
        return 0

    lax.fori_loop(0, blocks, one_block, 0)


def recur(
    core_ref,
    agg_ref,
    hgrad_ref,
    gcn_w_ref,
    gcn_b_ref,
    w_ref,
    bias_ref,
    w_back_ref,
    out_ref,
    keep_ref,
    send_ref,
    layer_s,
    slope_s,
    gates_s,
    cell_s,
    squash_s,
    hprev_s,
    dgates_s,
    dpre_s,
    grads_s,
):
    steps, rows, width = agg_ref.shape
    hid = width

    def layer(t, _):
        pre = jnp.dot(agg_ref[t], gcn_w_ref[...], preferred_element_type=F32) + gcn_b_ref[...]
        squeeze = sigmoid(pre)
        layer_s[t] = (pre * squeeze).astype(BF16)
        slope_s[t] = squeeze * (1.0 + pre * (1.0 - squeeze))
        return 0

    lax.fori_loop(0, steps, layer, 0, unroll=4)

    hprev_s[0] = jnp.zeros((rows, hid), BF16)
    cell_s[0] = jnp.zeros((rows, hid), F32)

    def advance(t, _):
        both = jnp.concatenate([layer_s[t], hprev_s[t]], axis=1)
        pre = jnp.dot(both, w_ref[...], preferred_element_type=F32) + bias_ref[...]
        gate_in = sigmoid(pre[:, :hid])
        gate_keep = sigmoid(pre[:, hid : 2 * hid])
        gate_new = jnp.tanh(pre[:, 2 * hid : 3 * hid])
        gate_out = sigmoid(pre[:, 3 * hid :])
        cell = gate_keep * cell_s[t] + gate_in * gate_new
        squash = jnp.tanh(cell)
        out = (gate_out * squash).astype(BF16)
        gates_s[t, :, :hid] = gate_in
        gates_s[t, :, hid : 2 * hid] = gate_keep
        gates_s[t, :, 2 * hid : 3 * hid] = gate_new
        gates_s[t, :, 3 * hid :] = gate_out
        cell_s[t + 1] = cell
        squash_s[t] = squash
        hprev_s[t + 1] = out
        out_ref[t] = out
        return 0

    lax.fori_loop(0, steps, advance, 0, unroll=4)

    def retreat(k, carried):
        grad_cell, grad_back = carried
        t = steps - 1 - k
        gate_in = gates_s[t, :, :hid]
        gate_keep = gates_s[t, :, hid : 2 * hid]
        gate_new = gates_s[t, :, 2 * hid : 3 * hid]
        gate_out = gates_s[t, :, 3 * hid :]
        squash = squash_s[t]
        grad_total = hgrad_ref[t].astype(F32) + grad_back
        grad_cell = grad_cell + grad_total * gate_out * (1.0 - squash * squash)
        dgates = jnp.concatenate(
            [
                (grad_cell * gate_new * gate_in * (1.0 - gate_in)).astype(BF16),
                (grad_cell * cell_s[t] * gate_keep * (1.0 - gate_keep)).astype(BF16),
                (grad_cell * gate_in * (1.0 - gate_new * gate_new)).astype(BF16),
                (grad_total * squash * gate_out * (1.0 - gate_out)).astype(BF16),
            ],
            axis=1,
        )
        dgates_s[t] = dgates
        back = jnp.dot(dgates, w_back_ref[...], preferred_element_type=F32)
        grad_layer = back[:, :width].astype(BF16).astype(F32)
        dpre_s[t] = (grad_layer * slope_s[t]).astype(BF16)
        return grad_cell * gate_keep, back[:, width:]

    zero = jnp.zeros((rows, hid), F32)
    lax.fori_loop(0, steps, retreat, (zero, zero), unroll=4)

    flat_dgates = dgates_s[...].reshape(steps * rows, 4 * hid)
    flat_dpre = dpre_s[...].reshape(steps * rows, width)

    def over_rows(left, right):
        return lax.dot_general(
            left, right, (((0,), (0,)), ((), ())), preferred_element_type=F32
        )

    def put(at, value):
        height = value.shape[0]
        for k in range(value.shape[1] // LANES):
            grads_s[pl.ds(at + k * height, height), :] = value[:, k * LANES : (k + 1) * LANES]
        return at + value.shape[1] // LANES * height

    ones = jnp.ones((8, steps * rows), BF16)
    at = put(0, over_rows(layer_s[...].reshape(steps * rows, width), flat_dgates))
    at = put(at, over_rows(hprev_s[:steps].reshape(steps * rows, hid), flat_dgates))
    at = put(at, over_rows(agg_ref[...].reshape(steps * rows, width), flat_dpre))
    at = put(at, jnp.dot(ones, flat_dgates, preferred_element_type=F32))
    at = put(at, jnp.dot(ones, flat_dpre, preferred_element_type=F32))
    grads_s[pl.ds(at, grads_s.shape[0] - at), :] = jnp.zeros((grads_s.shape[0] - at, LANES), F32)
    half = keep_ref.shape[0]
    core = core_ref[0]
    keep_ref[...] = grads_s[pl.ds(pl.multiple_of(core * half, 8), half), :]
    send_ref[...] = grads_s[pl.ds(pl.multiple_of((1 - core) * half, 8), half), :]


def sum_pair(left_ref, right_ref, out_ref):
    out_ref[...] = (left_ref[...] + right_ref[...]).astype(out_ref.dtype)


def sum_parts(part_ref, out_ref):
    total = jnp.sum(part_ref[...].astype(F32), axis=0)
    out_ref[...] = jnp.broadcast_to(total.astype(out_ref.dtype)[None], out_ref.shape)


def unpack(core_ref, mine_ref, other_ref, *refs):
    out_refs, total_ref = refs[:-1], refs[-1]
    half = mine_ref.shape[0]
    core = core_ref[0]
    total_ref[pl.ds(pl.multiple_of(core * half, 8), half), :] = mine_ref[...].astype(F32)
    total_ref[pl.ds(pl.multiple_of((1 - core) * half, 8), half), :] = other_ref[...].astype(F32)
    at = 0
    for out_ref in out_refs:
        height, columns = out_ref.shape
        taken = max(height, 8)
        for k in range(columns // LANES):
            out_ref[:, k * LANES : (k + 1) * LANES] = total_ref[pl.ds(at, taken), :][:height]
            at += taken


def on_device(
    features,
    tile_vals,
    tile_cols,
    tile_count,
    gcn_weight,
    gcn_bias,
    input_weight,
    recur_weight,
    lstm_bias,
    hidden_grad,
):
    steps_dev, local_verts, width = features.shape
    blocks, slots, size = tile_vals.shape[1:4]
    hid = recur_weight.shape[0]
    n_vtx, n_snap = lax.axis_size(VTX), lax.axis_size(SNAP)
    steps, rows = steps_dev * n_snap, local_verts // n_snap
    n_scatter, n_round = lax.axis_size(SCATTER), lax.axis_size(ROUND)
    held_rows = (2 * 4 * hid + width) * width // LANES + 8 * (4 * hid + width) // LANES
    share = -(-held_rows // (2 * 8 * n_scatter)) * 8
    half_rows = n_scatter * share
    core = lax.axis_index(PAIR).astype(jnp.int32).reshape(1)
    smem = pl.BlockSpec(memory_space=pltpu.SMEM)
    vmem = pl.BlockSpec(memory_space=pltpu.VMEM)
    hbm = pl.BlockSpec(memory_space=pltpu.HBM)

    with jax.named_scope("requests"):
        need = pl.pallas_call(
            functools.partial(find_requests, per_peer=blocks),
            out_shape=jax.ShapeDtypeStruct((n_vtx, LANES), jnp.int32),
            in_specs=[vmem],
            out_specs=vmem,
            compiler_params=pltpu.CompilerParams(vmem_limit_bytes=8 * MIB),
            name="find_requests",
        )(tile_cols)
        held_features = staged(
            features.reshape(steps_dev, blocks, size, width), 50 * MIB, "stage_features"
        )
        want = lax.all_to_all(need, VTX, 0, 0, tiled=True)

    with jax.named_scope("feature_blocks"):
        send = pl.pallas_call(
            pack_blocks,
            out_shape=jax.ShapeDtypeStruct((n_vtx, steps_dev, size, width), BF16),
            in_specs=[smem, vmem, hbm],
            out_specs=vmem,
            compiler_params=pltpu.CompilerParams(vmem_limit_bytes=46 * MIB),
            name="pack_blocks",
        )(want, held_features, tile_vals)
        recv = lax.all_to_all(send, VTX, 0, 0, tiled=True)

    with jax.named_scope("aggregate"):
        aggregated = pl.pallas_call(
            functools.partial(aggregate, per_peer=blocks),
            out_shape=jax.ShapeDtypeStruct((blocks, steps_dev, size, width), BF16),
            in_specs=[smem, smem, vmem, vmem],
            out_specs=vmem,
            compiler_params=pltpu.CompilerParams(vmem_limit_bytes=8 * MIB),
            name="aggregate",
        )(tile_cols, tile_count, recv, tile_vals)

    with jax.named_scope("to_vertices"):
        by_step = lax.all_to_all(
            aggregated.reshape(n_snap, steps_dev, rows, width), SNAP, 0, 0, tiled=True
        ).reshape(steps, rows, width)

    with jax.named_scope("recurrence"):
        outs, keep, away = pl.pallas_call(
            recur,
            out_shape=(
                jax.ShapeDtypeStruct((steps, rows, hid), BF16),
                jax.ShapeDtypeStruct((half_rows, LANES), F32),
                jax.ShapeDtypeStruct((half_rows, LANES), F32),
            ),
            in_specs=[smem] + [vmem] * 7,
            out_specs=(vmem, vmem, vmem),
            scratch_shapes=[
                pltpu.VMEM((steps, rows, width), BF16),
                pltpu.VMEM((steps, rows, width), F32),
                pltpu.VMEM((steps, rows, 4 * hid), F32),
                pltpu.VMEM((steps + 1, rows, hid), F32),
                pltpu.VMEM((steps, rows, hid), F32),
                pltpu.VMEM((steps + 1, rows, hid), BF16),
                pltpu.VMEM((steps, rows, 4 * hid), BF16),
                pltpu.VMEM((steps, rows, width), BF16),
                pltpu.VMEM((2 * half_rows, LANES), F32),
            ],
            compiler_params=pltpu.CompilerParams(vmem_limit_bytes=40 * MIB),
            name="recurrence",
        )(
            core,
            by_step,
            jnp.transpose(hidden_grad[0], (1, 0, 2)),
            gcn_weight,
            gcn_bias[None],
            jnp.concatenate([input_weight, recur_weight], axis=0),
            lstm_bias[None],
            jnp.concatenate([input_weight.T, recur_weight.T], axis=1),
        )

    with jax.named_scope("gradient_sums"):
        part = pl.pallas_call(
            sum_pair,
            out_shape=jax.ShapeDtypeStruct((half_rows, LANES), BF16),
            in_specs=[vmem, vmem],
            out_specs=vmem,
            compiler_params=pltpu.CompilerParams(vmem_limit_bytes=8 * MIB),
            name="sum_pair",
        )(keep, lax.ppermute(away, PAIR, ((0, 1), (1, 0))))
        part = lax.all_to_all(
            part.reshape(n_scatter, share, LANES), SCATTER, 0, 0, tiled=True
        )
        part = pl.pallas_call(
            sum_parts,
            out_shape=jax.ShapeDtypeStruct((n_round, share, LANES), BF16),
            in_specs=[vmem],
            out_specs=vmem,
            compiler_params=pltpu.CompilerParams(vmem_limit_bytes=8 * MIB),
            name="sum_scattered",
        )(part)
        part = lax.all_to_all(part, ROUND, 0, 0, tiled=True)
        part = pl.pallas_call(
            sum_parts,
            out_shape=jax.ShapeDtypeStruct((n_scatter, share, LANES), BF16),
            in_specs=[vmem],
            out_specs=vmem,
            compiler_params=pltpu.CompilerParams(vmem_limit_bytes=8 * MIB),
            name="sum_round",
        )(part)
        mine = lax.all_to_all(part, SCATTER, 0, 0, tiled=True).reshape(half_rows, LANES)
        other = lax.ppermute(mine, PAIR, ((0, 1), (1, 0)))
        grad_input, grad_recur, grad_gcn, grad_bias, grad_gbias = pl.pallas_call(
            unpack,
            out_shape=tuple(
                jax.ShapeDtypeStruct(shape, F32)
                for shape in (
                    (width, 4 * hid),
                    (hid, 4 * hid),
                    (width, width),
                    (1, 4 * hid),
                    (1, width),
                )
            ),
            in_specs=[smem, vmem, vmem],
            out_specs=(vmem,) * 5,
            scratch_shapes=[pltpu.VMEM((2 * half_rows, LANES), F32)],
            compiler_params=pltpu.CompilerParams(vmem_limit_bytes=8 * MIB),
            name="unpack",
        )(core, mine, other)

    hidden_states = jnp.transpose(outs, (1, 0, 2))[None]
    return (hidden_states, grad_gcn, grad_gbias[0], grad_input, grad_recur, grad_bias[0])


def solution(mesh):
    fine = Mesh(mesh.devices.reshape(4, 2, 8, 4), ("y", "core", "z", "x"))
    return jax.shard_map(
        on_device,
        mesh=fine,
        in_specs=(
            P(SNAP, VTX, None),
            P(SNAP, VTX, None, None, None),
            P(SNAP, VTX, None),
            P(SNAP, VTX),
            P(),
            P(),
            P(),
            P(),
            P(),
            P(VTX, SNAP, None, None),
        ),
        out_specs=(P(VTX, SNAP, None, None), P(), P(), P(), P(), P()),
        check_vma=False,
    )
```

```python
import functools

import jax
import jax.numpy as jnp
from jax import lax
from jax.experimental import pallas as pl
from jax.experimental.pallas import tpu as pltpu
from jax.sharding import Mesh
from jax.sharding import PartitionSpec as P

BF16 = jnp.bfloat16
F32 = jnp.float32
MIB = 1024 * 1024
LANES = 128
VTX, SNAP = ("z", "x"), ("y", "core")
SCATTER, ROUND, PAIR = ("x", "y"), "z", "core"


def sigmoid(value):
    return 0.5 * jnp.tanh(0.5 * value) + 0.5


def find_requests(cols_ref, need_ref, *, per_peer):
    steps, blocks, slots = cols_ref.shape
    peers = need_ref.shape[0]
    peer_iota = lax.broadcasted_iota(jnp.int32, (peers, slots), 0)
    lane = lax.broadcasted_iota(jnp.int32, need_ref.shape, 1)
    need = jnp.zeros(need_ref.shape, jnp.int32)
    for step in range(steps):
        found = jnp.zeros((peers, slots), jnp.int32)
        for block in range(blocks):
            cols = jnp.broadcast_to(cols_ref[step, block : block + 1, :], (peers, slots))
            inner = cols - peer_iota * per_peer
            found = jnp.maximum(found, jnp.where(inner < per_peer, inner, 0))
        need = jnp.where(lane == step, jnp.max(found, axis=1, keepdims=True), need)
    need_ref[...] = need


def stage(from_ref, to_ref, sem):
    copy = pltpu.make_async_copy(from_ref, to_ref, sem)
    copy.start()
    copy.wait()


def staged(value, limit, name):
    return pl.pallas_call(
        stage,
        out_shape=jax.ShapeDtypeStruct(value.shape, value.dtype),
        in_specs=[pl.BlockSpec(memory_space=pltpu.HBM)],
        out_specs=pl.BlockSpec(memory_space=pltpu.VMEM),
        scratch_shapes=[pltpu.SemaphoreType.DMA],
        compiler_params=pltpu.CompilerParams(vmem_limit_bytes=limit),
        cost_estimate=pl.CostEstimate(
            flops=0, bytes_accessed=2 * value.size * value.dtype.itemsize, transcendentals=0
        ),
        name=name,
    )(value)


def pack_blocks(want_ref, feat_ref, tile_ref, send_ref):
    del tile_ref
    peers, steps = send_ref.shape[:2]
    per_peer = feat_ref.shape[1]

    def fill(peer, _):
        for step in range(steps):
            pick = jnp.clip(want_ref[peer, step], 0, per_peer - 1)
            send_ref[peer, step] = feat_ref[step, pick]
        return 0

    lax.fori_loop(0, peers, fill, 0, unroll=8)


def aggregate(cols_ref, count_ref, recv_ref, tile_ref, out_ref, *, per_peer):
    steps, blocks, slots, size = tile_ref.shape[:4]
    peers, width = recv_ref.shape[0], recv_ref.shape[3]

    def add_up(block, lives, taken):
        for step in range(steps):
            total = jnp.zeros((size, width), F32)
            for slot in range(0, taken, 2):
                tiles, held = [], []
                for at in (slot, slot + 1):
                    peer = jnp.clip(lax.div(cols_ref[step, block, at], per_peer), 0, peers - 1)
                    picked = recv_ref[peer, step]
                    tiles.append(tile_ref[step, block, at])
                    held.append(lax.select_n(at < lives[step], jnp.zeros_like(picked), picked))
                total = total + jnp.dot(
                    jnp.concatenate(tiles, axis=1),
                    jnp.concatenate(held, axis=0),
                    preferred_element_type=F32,
                )
            out_ref[block, step] = total.astype(BF16)

    def one_block(block, _):
        lives = [count_ref[step, block] for step in range(steps)]
        few = functools.reduce(jnp.maximum, lives) <= slots // 2
        pl.when(few)(lambda: add_up(block, lives, slots // 2))
        pl.when(jnp.logical_not(few))(lambda: add_up(block, lives, slots))
        return 0

    lax.fori_loop(0, blocks, one_block, 0)


def recur(
    core_ref,
    agg_ref,
    hgrad_ref,
    gcn_w_ref,
    gcn_b_ref,
    w_ref,
    bias_ref,
    w_back_ref,
    out_ref,
    keep_ref,
    send_ref,
    layer_s,
    slope_s,
    gates_s,
    cell_s,
    squash_s,
    hprev_s,
    dgates_s,
    dpre_s,
    grads_s,
):
    steps, rows, width = agg_ref.shape
    hid = width

    def layer(t, _):
        pre = jnp.dot(agg_ref[t], gcn_w_ref[...], preferred_element_type=F32) + gcn_b_ref[...]
        squeeze = sigmoid(pre)
        layer_s[t] = (pre * squeeze).astype(BF16)
        slope_s[t] = squeeze * (1.0 + pre * (1.0 - squeeze))
        return 0

    lax.fori_loop(0, steps, layer, 0, unroll=4)

    hprev_s[0] = jnp.zeros((rows, hid), BF16)
    cell_s[0] = jnp.zeros((rows, hid), F32)

    def advance(t, _):
        both = jnp.concatenate([layer_s[t], hprev_s[t]], axis=1)
        pre = jnp.dot(both, w_ref[...], preferred_element_type=F32) + bias_ref[...]
        gate_in = sigmoid(pre[:, :hid])
        gate_keep = sigmoid(pre[:, hid : 2 * hid])
        gate_new = jnp.tanh(pre[:, 2 * hid : 3 * hid])
        gate_out = sigmoid(pre[:, 3 * hid :])
        cell = gate_keep * cell_s[t] + gate_in * gate_new
        squash = jnp.tanh(cell)
        out = (gate_out * squash).astype(BF16)
        gates_s[t, :, :hid] = gate_in
        gates_s[t, :, hid : 2 * hid] = gate_keep
        gates_s[t, :, 2 * hid : 3 * hid] = gate_new
        gates_s[t, :, 3 * hid :] = gate_out
        cell_s[t + 1] = cell
        squash_s[t] = squash
        hprev_s[t + 1] = out
        out_ref[t] = out
        return 0

    lax.fori_loop(0, steps, advance, 0, unroll=8)

    def retreat(k, carried):
        grad_cell, grad_back = carried
        t = steps - 1 - k
        gate_in = gates_s[t, :, :hid]
        gate_keep = gates_s[t, :, hid : 2 * hid]
        gate_new = gates_s[t, :, 2 * hid : 3 * hid]
        gate_out = gates_s[t, :, 3 * hid :]
        squash = squash_s[t]
        grad_total = hgrad_ref[t].astype(F32) + grad_back
        grad_cell = grad_cell + grad_total * gate_out * (1.0 - squash * squash)
        dgates = jnp.concatenate(
            [
                (grad_cell * gate_new * gate_in * (1.0 - gate_in)).astype(BF16),
                (grad_cell * cell_s[t] * gate_keep * (1.0 - gate_keep)).astype(BF16),
                (grad_cell * gate_in * (1.0 - gate_new * gate_new)).astype(BF16),
                (grad_total * squash * gate_out * (1.0 - gate_out)).astype(BF16),
            ],
            axis=1,
        )
        dgates_s[t] = dgates
        back = jnp.dot(dgates, w_back_ref[...], preferred_element_type=F32)
        grad_layer = back[:, :width].astype(BF16).astype(F32)
        dpre_s[t] = (grad_layer * slope_s[t]).astype(BF16)
        return grad_cell * gate_keep, back[:, width:]

    zero = jnp.zeros((rows, hid), F32)
    lax.fori_loop(0, steps, retreat, (zero, zero), unroll=8)

    flat_dgates = dgates_s[...].reshape(steps * rows, 4 * hid)
    flat_dpre = dpre_s[...].reshape(steps * rows, width)

    def over_rows(left, right):
        return lax.dot_general(
            left, right, (((0,), (0,)), ((), ())), preferred_element_type=F32
        )

    def put(at, value):
        height = value.shape[0]
        for k in range(value.shape[1] // LANES):
            grads_s[pl.ds(at + k * height, height), :] = value[:, k * LANES : (k + 1) * LANES]
        return at + value.shape[1] // LANES * height

    ones = jnp.ones((8, steps * rows), BF16)
    at = put(0, over_rows(layer_s[...].reshape(steps * rows, width), flat_dgates))
    at = put(at, over_rows(hprev_s[:steps].reshape(steps * rows, hid), flat_dgates))
    at = put(at, over_rows(agg_ref[...].reshape(steps * rows, width), flat_dpre))
    at = put(at, jnp.dot(ones, flat_dgates, preferred_element_type=F32))
    at = put(at, jnp.dot(ones, flat_dpre, preferred_element_type=F32))
    grads_s[pl.ds(at, grads_s.shape[0] - at), :] = jnp.zeros((grads_s.shape[0] - at, LANES), F32)
    half = keep_ref.shape[0]
    core = core_ref[0]
    keep_ref[...] = grads_s[pl.ds(pl.multiple_of(core * half, 8), half), :]
    send_ref[...] = grads_s[pl.ds(pl.multiple_of((1 - core) * half, 8), half), :]


def sum_pair(left_ref, right_ref, out_ref):
    out_ref[...] = (left_ref[...] + right_ref[...]).astype(out_ref.dtype)


def sum_parts(part_ref, out_ref):
    total = jnp.sum(part_ref[...].astype(F32), axis=0)
    out_ref[...] = jnp.broadcast_to(total.astype(out_ref.dtype)[None], out_ref.shape)


def unpack(core_ref, mine_ref, other_ref, *refs):
    out_refs, total_ref = refs[:-1], refs[-1]
    half = mine_ref.shape[0]
    core = core_ref[0]
    total_ref[pl.ds(pl.multiple_of(core * half, 8), half), :] = mine_ref[...].astype(F32)
    total_ref[pl.ds(pl.multiple_of((1 - core) * half, 8), half), :] = other_ref[...].astype(F32)
    at = 0
    for out_ref in out_refs:
        height, columns = out_ref.shape
        taken = max(height, 8)
        for k in range(columns // LANES):
            out_ref[:, k * LANES : (k + 1) * LANES] = total_ref[pl.ds(at, taken), :][:height]
            at += taken


def on_device(
    features,
    tile_vals,
    tile_cols,
    tile_count,
    gcn_weight,
    gcn_bias,
    input_weight,
    recur_weight,
    lstm_bias,
    hidden_grad,
):
    steps_dev, local_verts, width = features.shape
    blocks, slots, size = tile_vals.shape[1:4]
    hid = recur_weight.shape[0]
    n_vtx, n_snap = lax.axis_size(VTX), lax.axis_size(SNAP)
    steps, rows = steps_dev * n_snap, local_verts // n_snap
    n_scatter, n_round = lax.axis_size(SCATTER), lax.axis_size(ROUND)
    held_rows = (2 * 4 * hid + width) * width // LANES + 8 * (4 * hid + width) // LANES
    share = -(-held_rows // (2 * 8 * n_scatter)) * 8
    half_rows = n_scatter * share
    core = lax.axis_index(PAIR).astype(jnp.int32).reshape(1)
    smem = pl.BlockSpec(memory_space=pltpu.SMEM)
    vmem = pl.BlockSpec(memory_space=pltpu.VMEM)
    hbm = pl.BlockSpec(memory_space=pltpu.HBM)

    with jax.named_scope("requests"):
        need = pl.pallas_call(
            functools.partial(find_requests, per_peer=blocks),
            out_shape=jax.ShapeDtypeStruct((n_vtx, LANES), jnp.int32),
            in_specs=[vmem],
            out_specs=vmem,
            compiler_params=pltpu.CompilerParams(vmem_limit_bytes=8 * MIB),
            name="find_requests",
        )(tile_cols)
        held_features = staged(
            features.reshape(steps_dev, blocks, size, width), 50 * MIB, "stage_features"
        )
        want = lax.all_to_all(need, VTX, 0, 0, tiled=True)

    with jax.named_scope("feature_blocks"):
        send = pl.pallas_call(
            pack_blocks,
            out_shape=jax.ShapeDtypeStruct((n_vtx, steps_dev, size, width), BF16),
            in_specs=[smem, vmem, hbm],
            out_specs=vmem,
            compiler_params=pltpu.CompilerParams(vmem_limit_bytes=46 * MIB),
            name="pack_blocks",
        )(want, held_features, tile_vals)
        recv = lax.all_to_all(send, VTX, 0, 0, tiled=True)

    with jax.named_scope("aggregate"):
        aggregated = pl.pallas_call(
            functools.partial(aggregate, per_peer=blocks),
            out_shape=jax.ShapeDtypeStruct((blocks, steps_dev, size, width), BF16),
            in_specs=[smem, smem, vmem, vmem],
            out_specs=vmem,
            compiler_params=pltpu.CompilerParams(vmem_limit_bytes=8 * MIB),
            name="aggregate",
        )(tile_cols, tile_count, recv, tile_vals)

    with jax.named_scope("to_vertices"):
        by_step = lax.all_to_all(
            aggregated.reshape(n_snap, steps_dev, rows, width), SNAP, 0, 0, tiled=True
        ).reshape(steps, rows, width)

    with jax.named_scope("recurrence"):
        outs, keep, away = pl.pallas_call(
            recur,
            out_shape=(
                jax.ShapeDtypeStruct((steps, rows, hid), BF16),
                jax.ShapeDtypeStruct((half_rows, LANES), F32),
                jax.ShapeDtypeStruct((half_rows, LANES), F32),
            ),
            in_specs=[smem] + [vmem] * 7,
            out_specs=(vmem, vmem, vmem),
            scratch_shapes=[
                pltpu.VMEM((steps, rows, width), BF16),
                pltpu.VMEM((steps, rows, width), F32),
                pltpu.VMEM((steps, rows, 4 * hid), F32),
                pltpu.VMEM((steps + 1, rows, hid), F32),
                pltpu.VMEM((steps, rows, hid), F32),
                pltpu.VMEM((steps + 1, rows, hid), BF16),
                pltpu.VMEM((steps, rows, 4 * hid), BF16),
                pltpu.VMEM((steps, rows, width), BF16),
                pltpu.VMEM((2 * half_rows, LANES), F32),
            ],
            compiler_params=pltpu.CompilerParams(vmem_limit_bytes=40 * MIB),
            name="recurrence",
        )(
            core,
            by_step,
            jnp.transpose(hidden_grad[0], (1, 0, 2)),
            gcn_weight,
            gcn_bias[None],
            jnp.concatenate([input_weight, recur_weight], axis=0),
            lstm_bias[None],
            jnp.concatenate([input_weight.T, recur_weight.T], axis=1),
        )

    with jax.named_scope("gradient_sums"):
        part = pl.pallas_call(
            sum_pair,
            out_shape=jax.ShapeDtypeStruct((half_rows, LANES), BF16),
            in_specs=[vmem, vmem],
            out_specs=vmem,
            compiler_params=pltpu.CompilerParams(vmem_limit_bytes=8 * MIB),
            name="sum_pair",
        )(keep, lax.ppermute(away, PAIR, ((0, 1), (1, 0))))
        part = lax.all_to_all(
            part.reshape(n_scatter, share, LANES), SCATTER, 0, 0, tiled=True
        )
        part = pl.pallas_call(
            sum_parts,
            out_shape=jax.ShapeDtypeStruct((n_round, share, LANES), BF16),
            in_specs=[vmem],
            out_specs=vmem,
            compiler_params=pltpu.CompilerParams(vmem_limit_bytes=8 * MIB),
            name="sum_scattered",
        )(part)
        part = lax.all_to_all(part, ROUND, 0, 0, tiled=True)
        part = pl.pallas_call(
            sum_parts,
            out_shape=jax.ShapeDtypeStruct((n_scatter, share, LANES), BF16),
            in_specs=[vmem],
            out_specs=vmem,
            compiler_params=pltpu.CompilerParams(vmem_limit_bytes=8 * MIB),
            name="sum_round",
        )(part)
        mine = lax.all_to_all(part, SCATTER, 0, 0, tiled=True).reshape(half_rows, LANES)
        other = lax.ppermute(mine, PAIR, ((0, 1), (1, 0)))
        grad_input, grad_recur, grad_gcn, grad_bias, grad_gbias = pl.pallas_call(
            unpack,
            out_shape=tuple(
                jax.ShapeDtypeStruct(shape, F32)
                for shape in (
                    (width, 4 * hid),
                    (hid, 4 * hid),
                    (width, width),
                    (1, 4 * hid),
                    (1, width),
                )
            ),
            in_specs=[smem, vmem, vmem],
            out_specs=(vmem,) * 5,
            scratch_shapes=[pltpu.VMEM((2 * half_rows, LANES), F32)],
            compiler_params=pltpu.CompilerParams(vmem_limit_bytes=8 * MIB),
            name="unpack",
        )(core, mine, other)

    hidden_states = jnp.transpose(outs, (1, 0, 2))[None]
    return (hidden_states, grad_gcn, grad_gbias[0], grad_input, grad_recur, grad_bias[0])


def solution(mesh):
    fine = Mesh(mesh.devices.reshape(4, 2, 8, 4), ("y", "core", "z", "x"))
    return jax.shard_map(
        on_device,
        mesh=fine,
        in_specs=(
            P(SNAP, VTX, None),
            P(SNAP, VTX, None, None, None),
            P(SNAP, VTX, None),
            P(SNAP, VTX),
            P(),
            P(),
            P(),
            P(),
            P(),
            P(VTX, SNAP, None, None),
        ),
        out_specs=(P(VTX, SNAP, None, None), P(), P(), P(), P(), P()),
        check_vma=False,
    )
```

```python
import functools

import jax
import jax.numpy as jnp
from jax import lax
from jax.experimental import pallas as pl
from jax.experimental.pallas import tpu as pltpu
from jax.sharding import Mesh
from jax.sharding import PartitionSpec as P

BF16 = jnp.bfloat16
F32 = jnp.float32
MIB = 1024 * 1024
LANES = 128
VTX, SNAP = ("z", "x"), ("y", "core")
SCATTER, ROUND, PAIR = ("x", "y"), "z", "core"


def sigmoid(value):
    return 0.5 * jnp.tanh(0.5 * value) + 0.5


def find_requests(cols_ref, need_ref, *, per_peer):
    steps, blocks, slots = cols_ref.shape
    peers = need_ref.shape[0]
    peer_iota = lax.broadcasted_iota(jnp.int32, (peers, slots), 0)
    lane = lax.broadcasted_iota(jnp.int32, need_ref.shape, 1)
    need = jnp.zeros(need_ref.shape, jnp.int32)
    for step in range(steps):
        found = jnp.zeros((peers, slots), jnp.int32)
        for block in range(blocks):
            cols = jnp.broadcast_to(cols_ref[step, block : block + 1, :], (peers, slots))
            inner = cols - peer_iota * per_peer
            found = jnp.maximum(found, jnp.where(inner < per_peer, inner, 0))
        need = jnp.where(lane == step, jnp.max(found, axis=1, keepdims=True), need)
    need_ref[...] = need


def stage(from_ref, to_ref, sem):
    copy = pltpu.make_async_copy(from_ref, to_ref, sem)
    copy.start()
    copy.wait()


def staged(value, limit, name):
    return pl.pallas_call(
        stage,
        out_shape=jax.ShapeDtypeStruct(value.shape, value.dtype),
        in_specs=[pl.BlockSpec(memory_space=pltpu.HBM)],
        out_specs=pl.BlockSpec(memory_space=pltpu.VMEM),
        scratch_shapes=[pltpu.SemaphoreType.DMA],
        compiler_params=pltpu.CompilerParams(vmem_limit_bytes=limit),
        cost_estimate=pl.CostEstimate(
            flops=0, bytes_accessed=2 * value.size * value.dtype.itemsize, transcendentals=0
        ),
        name=name,
    )(value)


def pack_blocks(want_ref, feat_ref, tile_ref, send_ref):
    del tile_ref
    peers, steps = send_ref.shape[:2]
    per_peer = feat_ref.shape[1]

    def fill(peer, _):
        for step in range(steps):
            pick = jnp.clip(want_ref[peer, step], 0, per_peer - 1)
            send_ref[peer, step] = feat_ref[step, pick]
        return 0

    lax.fori_loop(0, peers, fill, 0, unroll=8)


def aggregate(cols_ref, count_ref, recv_ref, tile_ref, out_ref, *, per_peer):
    steps, blocks, slots, size = tile_ref.shape[:4]
    peers, width = recv_ref.shape[0], recv_ref.shape[3]

    def add_up(block, lives, taken):
        for step in range(steps):
            total = jnp.zeros((size, width), F32)
            for slot in range(0, taken, 2):
                tiles, held = [], []
                for at in (slot, slot + 1):
                    peer = jnp.clip(lax.div(cols_ref[step, block, at], per_peer), 0, peers - 1)
                    picked = recv_ref[peer, step]
                    tiles.append(tile_ref[step, block, at])
                    held.append(lax.select_n(at < lives[step], jnp.zeros_like(picked), picked))
                total = total + jnp.dot(
                    jnp.concatenate(tiles, axis=1),
                    jnp.concatenate(held, axis=0),
                    preferred_element_type=F32,
                )
            out_ref[block, step] = total.astype(BF16)

    def one_block(block, _):
        lives = [count_ref[step, block] for step in range(steps)]
        few = functools.reduce(jnp.maximum, lives) <= slots // 2
        pl.when(few)(lambda: add_up(block, lives, slots // 2))
        pl.when(jnp.logical_not(few))(lambda: add_up(block, lives, slots))
        return 0

    lax.fori_loop(0, blocks, one_block, 0)


def recur(
    core_ref,
    agg_ref,
    hgrad_ref,
    gcn_w_ref,
    gcn_b_ref,
    w_ref,
    bias_ref,
    w_back_ref,
    out_ref,
    keep_ref,
    send_ref,
    layer_s,
    slope_s,
    gates_s,
    cell_s,
    squash_s,
    hprev_s,
    dgates_s,
    dpre_s,
    grads_s,
):
    steps, rows, width = agg_ref.shape
    hid = width

    def layer(t, _):
        pre = jnp.dot(agg_ref[t], gcn_w_ref[...], preferred_element_type=F32) + gcn_b_ref[...]
        squeeze = sigmoid(pre)
        layer_s[t] = (pre * squeeze).astype(BF16)
        slope_s[t] = squeeze * (1.0 + pre * (1.0 - squeeze))
        return 0

    lax.fori_loop(0, steps, layer, 0, unroll=8)

    hprev_s[0] = jnp.zeros((rows, hid), BF16)
    cell_s[0] = jnp.zeros((rows, hid), F32)

    def advance(t, _):
        both = jnp.concatenate([layer_s[t], hprev_s[t]], axis=1)
        pre = jnp.dot(both, w_ref[...], preferred_element_type=F32) + bias_ref[...]
        gate_in = sigmoid(pre[:, :hid])
        gate_keep = sigmoid(pre[:, hid : 2 * hid])
        gate_new = jnp.tanh(pre[:, 2 * hid : 3 * hid])
        gate_out = sigmoid(pre[:, 3 * hid :])
        cell = gate_keep * cell_s[t] + gate_in * gate_new
        squash = jnp.tanh(cell)
        out = (gate_out * squash).astype(BF16)
        gates_s[t, :, :hid] = gate_in
        gates_s[t, :, hid : 2 * hid] = gate_keep
        gates_s[t, :, 2 * hid : 3 * hid] = gate_new
        gates_s[t, :, 3 * hid :] = gate_out
        cell_s[t + 1] = cell
        squash_s[t] = squash
        hprev_s[t + 1] = out
        out_ref[t] = out
        return 0

    lax.fori_loop(0, steps, advance, 0, unroll=8)

    def retreat(k, carried):
        grad_cell, grad_back = carried
        t = steps - 1 - k
        gate_in = gates_s[t, :, :hid]
        gate_keep = gates_s[t, :, hid : 2 * hid]
        gate_new = gates_s[t, :, 2 * hid : 3 * hid]
        gate_out = gates_s[t, :, 3 * hid :]
        squash = squash_s[t]
        grad_total = hgrad_ref[t].astype(F32) + grad_back
        grad_cell = grad_cell + grad_total * gate_out * (1.0 - squash * squash)
        dgates = jnp.concatenate(
            [
                (grad_cell * gate_new * gate_in * (1.0 - gate_in)).astype(BF16),
                (grad_cell * cell_s[t] * gate_keep * (1.0 - gate_keep)).astype(BF16),
                (grad_cell * gate_in * (1.0 - gate_new * gate_new)).astype(BF16),
                (grad_total * squash * gate_out * (1.0 - gate_out)).astype(BF16),
            ],
            axis=1,
        )
        dgates_s[t] = dgates
        back = jnp.dot(dgates, w_back_ref[...], preferred_element_type=F32)
        grad_layer = back[:, :width].astype(BF16).astype(F32)
        dpre_s[t] = (grad_layer * slope_s[t]).astype(BF16)
        return grad_cell * gate_keep, back[:, width:]

    zero = jnp.zeros((rows, hid), F32)
    lax.fori_loop(0, steps, retreat, (zero, zero), unroll=8)

    flat_dgates = dgates_s[...].reshape(steps * rows, 4 * hid)
    flat_dpre = dpre_s[...].reshape(steps * rows, width)

    def over_rows(left, right):
        return lax.dot_general(
            left, right, (((0,), (0,)), ((), ())), preferred_element_type=F32
        )

    def put(at, value):
        height = value.shape[0]
        for k in range(value.shape[1] // LANES):
            grads_s[pl.ds(at + k * height, height), :] = value[:, k * LANES : (k + 1) * LANES]
        return at + value.shape[1] // LANES * height

    ones = jnp.ones((8, steps * rows), BF16)
    at = put(0, over_rows(layer_s[...].reshape(steps * rows, width), flat_dgates))
    at = put(at, over_rows(hprev_s[:steps].reshape(steps * rows, hid), flat_dgates))
    at = put(at, over_rows(agg_ref[...].reshape(steps * rows, width), flat_dpre))
    at = put(at, jnp.dot(ones, flat_dgates, preferred_element_type=F32))
    at = put(at, jnp.dot(ones, flat_dpre, preferred_element_type=F32))
    grads_s[pl.ds(at, grads_s.shape[0] - at), :] = jnp.zeros((grads_s.shape[0] - at, LANES), F32)
    half = keep_ref.shape[0]
    core = core_ref[0]
    keep_ref[...] = grads_s[pl.ds(pl.multiple_of(core * half, 8), half), :]
    send_ref[...] = grads_s[pl.ds(pl.multiple_of((1 - core) * half, 8), half), :]


def sum_pair(left_ref, right_ref, out_ref):
    out_ref[...] = (left_ref[...] + right_ref[...]).astype(out_ref.dtype)


def sum_parts(part_ref, out_ref):
    total = jnp.sum(part_ref[...].astype(F32), axis=0)
    out_ref[...] = jnp.broadcast_to(total.astype(out_ref.dtype)[None], out_ref.shape)


def unpack(core_ref, mine_ref, other_ref, *refs):
    out_refs, total_ref = refs[:-1], refs[-1]
    half = mine_ref.shape[0]
    core = core_ref[0]
    total_ref[pl.ds(pl.multiple_of(core * half, 8), half), :] = mine_ref[...].astype(F32)
    total_ref[pl.ds(pl.multiple_of((1 - core) * half, 8), half), :] = other_ref[...].astype(F32)
    at = 0
    for out_ref in out_refs:
        height, columns = out_ref.shape
        taken = max(height, 8)
        for k in range(columns // LANES):
            out_ref[:, k * LANES : (k + 1) * LANES] = total_ref[pl.ds(at, taken), :][:height]
            at += taken


def on_device(
    features,
    tile_vals,
    tile_cols,
    tile_count,
    gcn_weight,
    gcn_bias,
    input_weight,
    recur_weight,
    lstm_bias,
    hidden_grad,
):
    steps_dev, local_verts, width = features.shape
    blocks, slots, size = tile_vals.shape[1:4]
    hid = recur_weight.shape[0]
    n_vtx, n_snap = lax.axis_size(VTX), lax.axis_size(SNAP)
    steps, rows = steps_dev * n_snap, local_verts // n_snap
    n_scatter, n_round = lax.axis_size(SCATTER), lax.axis_size(ROUND)
    held_rows = (2 * 4 * hid + width) * width // LANES + 8 * (4 * hid + width) // LANES
    share = -(-held_rows // (2 * 8 * n_scatter)) * 8
    half_rows = n_scatter * share
    core = lax.axis_index(PAIR).astype(jnp.int32).reshape(1)
    smem = pl.BlockSpec(memory_space=pltpu.SMEM)
    vmem = pl.BlockSpec(memory_space=pltpu.VMEM)
    hbm = pl.BlockSpec(memory_space=pltpu.HBM)

    with jax.named_scope("requests"):
        need = pl.pallas_call(
            functools.partial(find_requests, per_peer=blocks),
            out_shape=jax.ShapeDtypeStruct((n_vtx, LANES), jnp.int32),
            in_specs=[vmem],
            out_specs=vmem,
            compiler_params=pltpu.CompilerParams(vmem_limit_bytes=8 * MIB),
            name="find_requests",
        )(tile_cols)
        held_features = staged(
            features.reshape(steps_dev, blocks, size, width), 50 * MIB, "stage_features"
        )
        want = lax.all_to_all(need, VTX, 0, 0, tiled=True)

    with jax.named_scope("feature_blocks"):
        send = pl.pallas_call(
            pack_blocks,
            out_shape=jax.ShapeDtypeStruct((n_vtx, steps_dev, size, width), BF16),
            in_specs=[smem, vmem, hbm],
            out_specs=vmem,
            compiler_params=pltpu.CompilerParams(vmem_limit_bytes=46 * MIB),
            name="pack_blocks",
        )(want, held_features, tile_vals)
        recv = lax.all_to_all(send, VTX, 0, 0, tiled=True)

    with jax.named_scope("aggregate"):
        aggregated = pl.pallas_call(
            functools.partial(aggregate, per_peer=blocks),
            out_shape=jax.ShapeDtypeStruct((blocks, steps_dev, size, width), BF16),
            in_specs=[smem, smem, vmem, vmem],
            out_specs=vmem,
            compiler_params=pltpu.CompilerParams(vmem_limit_bytes=8 * MIB),
            name="aggregate",
        )(tile_cols, tile_count, recv, tile_vals)

    with jax.named_scope("to_vertices"):
        by_step = lax.all_to_all(
            aggregated.reshape(n_snap, steps_dev, rows, width), SNAP, 0, 0, tiled=True
        ).reshape(steps, rows, width)

    with jax.named_scope("recurrence"):
        outs, keep, away = pl.pallas_call(
            recur,
            out_shape=(
                jax.ShapeDtypeStruct((steps, rows, hid), BF16),
                jax.ShapeDtypeStruct((half_rows, LANES), F32),
                jax.ShapeDtypeStruct((half_rows, LANES), F32),
            ),
            in_specs=[smem] + [vmem] * 7,
            out_specs=(vmem, vmem, vmem),
            scratch_shapes=[
                pltpu.VMEM((steps, rows, width), BF16),
                pltpu.VMEM((steps, rows, width), F32),
                pltpu.VMEM((steps, rows, 4 * hid), F32),
                pltpu.VMEM((steps + 1, rows, hid), F32),
                pltpu.VMEM((steps, rows, hid), F32),
                pltpu.VMEM((steps + 1, rows, hid), BF16),
                pltpu.VMEM((steps, rows, 4 * hid), BF16),
                pltpu.VMEM((steps, rows, width), BF16),
                pltpu.VMEM((2 * half_rows, LANES), F32),
            ],
            compiler_params=pltpu.CompilerParams(vmem_limit_bytes=40 * MIB),
            name="recurrence",
        )(
            core,
            by_step,
            jnp.transpose(hidden_grad[0], (1, 0, 2)),
            gcn_weight,
            gcn_bias[None],
            jnp.concatenate([input_weight, recur_weight], axis=0),
            lstm_bias[None],
            jnp.concatenate([input_weight.T, recur_weight.T], axis=1),
        )

    with jax.named_scope("gradient_sums"):
        part = pl.pallas_call(
            sum_pair,
            out_shape=jax.ShapeDtypeStruct((half_rows, LANES), BF16),
            in_specs=[vmem, vmem],
            out_specs=vmem,
            compiler_params=pltpu.CompilerParams(vmem_limit_bytes=8 * MIB),
            name="sum_pair",
        )(keep, lax.ppermute(away, PAIR, ((0, 1), (1, 0))))
        part = lax.all_to_all(
            part.reshape(n_scatter, share, LANES), SCATTER, 0, 0, tiled=True
        )
        part = pl.pallas_call(
            sum_parts,
            out_shape=jax.ShapeDtypeStruct((n_round, share, LANES), BF16),
            in_specs=[vmem],
            out_specs=vmem,
            compiler_params=pltpu.CompilerParams(vmem_limit_bytes=8 * MIB),
            name="sum_scattered",
        )(part)
        part = lax.all_to_all(part, ROUND, 0, 0, tiled=True)
        part = pl.pallas_call(
            sum_parts,
            out_shape=jax.ShapeDtypeStruct((n_scatter, share, LANES), BF16),
            in_specs=[vmem],
            out_specs=vmem,
            compiler_params=pltpu.CompilerParams(vmem_limit_bytes=8 * MIB),
            name="sum_round",
        )(part)
        mine = lax.all_to_all(part, SCATTER, 0, 0, tiled=True).reshape(half_rows, LANES)
        other = lax.ppermute(mine, PAIR, ((0, 1), (1, 0)))
        grad_input, grad_recur, grad_gcn, grad_bias, grad_gbias = pl.pallas_call(
            unpack,
            out_shape=tuple(
                jax.ShapeDtypeStruct(shape, F32)
                for shape in (
                    (width, 4 * hid),
                    (hid, 4 * hid),
                    (width, width),
                    (1, 4 * hid),
                    (1, width),
                )
            ),
            in_specs=[smem, vmem, vmem],
            out_specs=(vmem,) * 5,
            scratch_shapes=[pltpu.VMEM((2 * half_rows, LANES), F32)],
            compiler_params=pltpu.CompilerParams(vmem_limit_bytes=8 * MIB),
            name="unpack",
        )(core, mine, other)

    hidden_states = jnp.transpose(outs, (1, 0, 2))[None]
    return (hidden_states, grad_gcn, grad_gbias[0], grad_input, grad_recur, grad_bias[0])


def solution(mesh):
    fine = Mesh(mesh.devices.reshape(4, 2, 8, 4), ("y", "core", "z", "x"))
    return jax.shard_map(
        on_device,
        mesh=fine,
        in_specs=(
            P(SNAP, VTX, None),
            P(SNAP, VTX, None, None, None),
            P(SNAP, VTX, None),
            P(SNAP, VTX),
            P(),
            P(),
            P(),
            P(),
            P(),
            P(VTX, SNAP, None, None),
        ),
        out_specs=(P(VTX, SNAP, None, None), P(), P(), P(), P(), P()),
        check_vma=False,
    )
```
